32 devices in a mesh: seq: 8 (over z, y), tensor: 4 (over x, core).
Axes of the slice: x: 2, y: 2, z: 4, core: 2. Of those that a mesh axis runs over, the one named last changes fastest.
Arguments:
- residual: bfloat16 [4608, 6144], P('seq', 'tensor'), may hold values from -4 to 4
- queries: bfloat16 [4608, 4096], P(('seq', 'tensor')), may hold values from -6 to 6
- key_rows: bfloat16 [4608, 4096], P(('seq', 'tensor')), may hold values from -6 to 6
- value_rows: bfloat16 [4608, 4096], P(('seq', 'tensor')), may hold values from -6 to 6
- w_out: bfloat16 [4096, 6144], P(None, 'tensor'), may hold values from -0.09375 to 0.09375
- out_gate: float32 [6144], P('tensor'), may hold values from 0.5 to 1.5
- extents: int32 [32, 3], replicated, may hold values from 0 to 1, as said below
Outputs:
- updated: bfloat16 [4608, 6144], P('seq', 'tensor')
The draws below stay inside these ranges and needn't reach their ends.
Inputs may be any that keep to these rules, and one draw needn't show every extreme that they name: `extents`: reaches in tile-frames are at most 1, in tile-rows at most 1, in tile-columns at most 1; each of these bounds is taken by some head, and some head has reach 0 in tile-rows.
All inputs are finite; a program needn't handle non-finite values.
Results may differ from the reference program's by a relative error of at most 0.0048.
Values may be sent and summed in bfloat16 or wider, within the bound.
A program may use at most 192 MiB of HBM per device.

```python
import math
import jax
import jax.numpy as jnp
from jax import lax

D = 6144
HEAD_DIM = 128
HEADS = 32
TILE = 32
FT = 3
HT_DEV = 2
WT = 3
INNER = 4096
S_DEV = 576
TOKENS = 4608
N_SEQ = 8


def draw_pair(key):
    base_key = jax.random.fold_in(key, 71)
    key_q, key_k = jax.random.split(base_key, 2)
    query_part = jnp.clip(1.4 * jax.random.normal(key_q, (TOKENS, INNER), jnp.float32), -6.0, 6.0)
    key_part = jnp.clip(1.4 * jax.random.normal(key_k, (TOKENS, INNER), jnp.float32), -6.0, 6.0)
    return (query_part, key_part)


def draw_queries(key, part):
    return draw_pair(key)[0].astype(jnp.bfloat16)


def draw_key_rows(key, part):
    return draw_pair(key)[1].astype(jnp.bfloat16)


def draw_extents(key, part):
    base_key = jax.random.fold_in(key, 29)
    keys_all = jax.random.split(base_key, 6)
    head_ids = jnp.arange(HEADS, dtype=jnp.int32)
    frame_most = min(FT - 1, 1)
    col_most = min(WT - 1, 1)
    frames_reach = jax.random.randint(keys_all[0], (HEADS,), 0, frame_most + 1)
    rows_reach = jax.random.randint(keys_all[1], (HEADS,), 0, 2)
    cols_reach = jax.random.randint(keys_all[2], (HEADS,), 0, col_most + 1)
    pick_frame = jax.random.randint(keys_all[3], (), 0, HEADS)
    pick_row = jax.random.randint(keys_all[4], (), 0, HEADS)
    pick_col = jax.random.randint(keys_all[5], (), 0, HEADS)
    frames_reach = jnp.where(head_ids == pick_frame, frame_most, frames_reach)
    rows_reach = jnp.where(head_ids == (pick_row + 1) % HEADS, 0, rows_reach)
    rows_reach = jnp.where(head_ids == pick_row, 1, rows_reach)
    cols_reach = jnp.where(head_ids == pick_col, col_most, cols_reach)
    return jnp.stack([frames_reach, rows_reach, cols_reach], axis=1).astype(jnp.int32)


def block_levels(key, dims, cuts, least, largest):
    level, own = 1.0, jax.random.fold_in(key, 6)
    for axis_at, blocks in cuts:
        steps = jnp.exp(jax.random.uniform(jax.random.fold_in(own, axis_at), (blocks,), jnp.float32, least / len(cuts), largest / len(cuts)))
        level = level * jnp.repeat(steps, dims[axis_at] // blocks).reshape([-1 if axis == axis_at else 1 for axis in range(len(dims))])
    return level


def bell_draw(rng, extent, spread, reach, cuts=(), held_as=jnp.bfloat16):
    drawn = spread * jax.random.normal(rng, extent, jnp.float32)
    if cuts:
        drawn = drawn * block_levels(rng, extent, cuts, -0.22, 0.18)
    return jnp.clip(drawn, -reach, reach).astype(held_as)


def setup_inputs(seed: int = 0) -> dict:
    key_of = jax.random.split(jax.random.key(seed), 8)
    return {
        "residual": bell_draw(key_of[0], (TOKENS, D), 0.5, 4.0, ((0, 8), (1, 4))),
        "queries": draw_queries(jax.random.fold_in(key_of[7], 71), 0),
        "key_rows": draw_key_rows(jax.random.fold_in(key_of[7], 71), 0),
        "value_rows": bell_draw(key_of[3], (TOKENS, INNER), 1.0, 6.0, ((0, 32),)),
        "w_out": bell_draw(key_of[4], (INNER, D), INNER ** -0.5, 0.09375, ((1, 4),)),
        "out_gate": jnp.clip(0.5 + 1.0 * jax.random.uniform(key_of[5], (D,), jnp.float32) ** block_levels(key_of[5], (D,), ((0, 4),), -0.2, 0.2), 0.5, 1.5),
        "extents": draw_extents(jax.random.fold_in(key_of[7], 71), 0),
    }


def tile_coords(row_count, tile_rows, first_row):
    position = jnp.arange(row_count, dtype=jnp.int32)
    frame_id = position // (tile_rows * WT * TILE)
    row_id = first_row + position // (WT * TILE) % tile_rows
    col_id = position // TILE % WT
    return (frame_id, row_id, col_id)

def allowed_keys(query_place, key_place, head_reach, seq_block, seq_count):
    frame_gap = jnp.abs(query_place[0][:, None] - key_place[0][None, :])
    row_gap = jnp.abs(query_place[1][:, None] - key_place[1][None, :])
    col_gap = jnp.abs(query_place[2][:, None] - key_place[2][None, :])
    global_row = key_place[1] + seq_block * HT_DEV
    inside = (global_row >= 0) & (global_row < seq_count * HT_DEV)
    return (frame_gap[None] <= head_reach[:, 0, None, None]) & (row_gap[None] <= head_reach[:, 1, None, None]) & (col_gap[None] <= head_reach[:, 2, None, None]) & inside[None, None, :]

def reference(residual, queries, key_rows, value_rows, w_out, out_gate, extents):
    zero_rows = jnp.zeros((S_DEV, INNER), jnp.bfloat16)
    keys_padded = jnp.concatenate([zero_rows, key_rows, zero_rows], 0)
    values_padded = jnp.concatenate([zero_rows, value_rows, zero_rows], 0)
    query_place = tile_coords(S_DEV, HT_DEV, 0)
    three_parts = [tile_coords(S_DEV, HT_DEV, first) for first in (-HT_DEV, 0, HT_DEV)]
    key_place = tuple((jnp.concatenate([part[axis_id] for part in three_parts]) for axis_id in range(3)))

    def one_head(head_id):
        query_cols = lax.dynamic_slice_in_dim(queries, head_id * HEAD_DIM, HEAD_DIM, 1)
        key_cols = lax.dynamic_slice_in_dim(keys_padded, head_id * HEAD_DIM, HEAD_DIM, 1)
        value_cols = lax.dynamic_slice_in_dim(values_padded, head_id * HEAD_DIM, HEAD_DIM, 1)
        head_reach = lax.dynamic_slice_in_dim(extents, head_id, 1, 0)

        def one_block(seq_block):
            q_tile = lax.dynamic_slice_in_dim(query_cols, seq_block * S_DEV, S_DEV, 0)
            k_tile = lax.dynamic_slice_in_dim(key_cols, seq_block * S_DEV, 3 * S_DEV, 0)
            v_tile = lax.dynamic_slice_in_dim(value_cols, seq_block * S_DEV, 3 * S_DEV, 0)
            scores = jnp.dot(q_tile, k_tile.T, preferred_element_type=jnp.float32) / math.sqrt(HEAD_DIM)
            allowed = allowed_keys(query_place, key_place, head_reach, seq_block, N_SEQ)[0]
            scores = jnp.where(allowed, scores, -1e+30)
            row_max = lax.optimization_barrier(jnp.max(scores, axis=-1, keepdims=True))
            exp_scores = jnp.exp(scores - row_max)
            row_sum = lax.optimization_barrier(jnp.sum(exp_scores, axis=-1, keepdims=True))
            weights = (exp_scores / row_sum).astype(jnp.bfloat16)
            return jnp.dot(weights, v_tile, preferred_element_type=jnp.float32).astype(jnp.bfloat16)
        blocks = lax.map(one_block, jnp.arange(N_SEQ, dtype=jnp.int32))
        return blocks.reshape(TOKENS, HEAD_DIM)
    per_head = lax.map(one_head, jnp.arange(HEADS, dtype=jnp.int32))
    attended = per_head.transpose(1, 0, 2).reshape(TOKENS, INNER)
    projected = jnp.dot(attended, w_out, preferred_element_type=jnp.float32)
    return (residual.astype(jnp.float32) + out_gate * projected).astype(jnp.bfloat16)
```

```python
import functools
import math

import jax
import jax.numpy as jnp
import numpy as np
from jax import lax
from jax.experimental import pallas as pl
from jax.experimental.pallas import tpu as pltpu
from jax.sharding import PartitionSpec as P

HEAD_DIM = 128
TILE = 32
HT_DEV = 2
WT = 3
EARLY = 4
AHEAD = 3
OUT_TILE = 512
FAR = -1e30
MESH = pl.DeviceIdType.MESH


def passed_along(value, axis, by):
    length = lax.axis_size(axis)
    pairs = [(i, i + by) for i in range(length) if 0 <= i + by < length]
    return lax.ppermute(value, axis, pairs)


def tile_coords(row_count, tile_rows, first_row):
    position = jnp.arange(row_count, dtype=jnp.int32)
    frame_id = position // (tile_rows * WT * TILE)
    row_id = first_row + position // (WT * TILE) % tile_rows
    col_id = position // TILE % WT
    return (frame_id, row_id, col_id)


def allowed_keys(query_place, key_place, head_reach, seq_block, seq_count):
    frame_gap = jnp.abs(query_place[0][:, None] - key_place[0][None, :])
    row_gap = jnp.abs(query_place[1][:, None] - key_place[1][None, :])
    col_gap = jnp.abs(query_place[2][:, None] - key_place[2][None, :])
    global_row = key_place[1] + seq_block * HT_DEV
    inside = (global_row >= 0) & (global_row < seq_count * HT_DEV)
    return (
        (frame_gap[None] <= head_reach[:, 0, None, None])
        & (row_gap[None] <= head_reach[:, 1, None, None])
        & (col_gap[None] <= head_reach[:, 2, None, None])
        & inside[None, None, :]
    )


def plain_shards(residual, queries, key_rows, value_rows, w_out, out_gate, extents):
    head_q, head_k, head_v = (
        lax.all_to_all(queries, "tensor", split_axis=1, concat_axis=0, tiled=True),
        lax.all_to_all(key_rows, "tensor", split_axis=1, concat_axis=0, tiled=True),
        lax.all_to_all(value_rows, "tensor", split_axis=1, concat_axis=0, tiled=True),
    )
    tokens, inner_dev = head_q.shape
    heads_here = inner_dev // HEAD_DIM
    seq_block = lax.axis_index("seq")
    seq_count = lax.axis_size("seq")
    head_reach = lax.dynamic_slice_in_dim(
        extents, lax.axis_index("tensor") * heads_here, heads_here, 0
    )
    query_tiles = head_q.reshape(tokens, heads_here, HEAD_DIM)
    query_place = tile_coords(tokens, HT_DEV, 0)
    stacked = jnp.stack([head_k, head_v])

    def part_scores(pair_rows, key_place):
        key_tiles = pair_rows[0].reshape(-1, heads_here, HEAD_DIM)
        scores = jnp.einsum(
            "qhd,khd->hqk", query_tiles, key_tiles, preferred_element_type=jnp.float32
        ) / math.sqrt(HEAD_DIM)
        allowed = allowed_keys(query_place, key_place, head_reach, seq_block, seq_count)
        return jnp.where(allowed, scores, FAR)

    by_row = stacked.reshape(2, -1, HT_DEV, WT * TILE, inner_dev)
    halves = tokens // HT_DEV
    last_row = by_row[:, :, HT_DEV - 1].reshape(2, halves, inner_dev)
    first_row = by_row[:, :, 0].reshape(2, halves, inner_dev)
    parts = [
        (stacked, query_place),
        (passed_along(last_row, "seq", 1), tile_coords(halves, 1, -1)),
        (passed_along(first_row, "seq", -1), tile_coords(halves, 1, HT_DEV)),
    ]
    scores = jnp.concatenate([part_scores(*part) for part in parts], axis=-1)
    value_all = jnp.concatenate([pair_rows[1] for pair_rows, _ in parts], axis=0)
    row_max = jnp.max(scores, axis=-1, keepdims=True)
    exp_scores = jnp.exp(scores - row_max)
    row_sum = jnp.sum(exp_scores, axis=-1, keepdims=True)
    weights = (exp_scores / row_sum).astype(jnp.bfloat16)
    attended = jnp.einsum(
        "hqk,khd->qhd",
        weights,
        value_all.reshape(-1, heads_here, HEAD_DIM),
        preferred_element_type=jnp.float32,
    )
    head_out = attended.reshape(tokens, inner_dev).astype(jnp.bfloat16)
    projected = jnp.dot(
        lax.all_gather(head_out, "tensor", axis=1, tiled=True),
        w_out,
        preferred_element_type=jnp.float32,
    )
    return (residual.astype(jnp.float32) + out_gate * projected).astype(jnp.bfloat16)


def mask_features(frames):
    span = WT * TILE
    q_feat = np.zeros((2, frames * span, HEAD_DIM), np.float32)
    k_feat = np.zeros((2, frames * 3 * span, HEAD_DIM), np.float32)
    q_at = np.arange(frames * span)
    q_frame, q_col = q_at // span, q_at // TILE % WT
    k_at = np.arange(frames * 3 * span)
    k_frame, k_col = k_at // (3 * span), k_at // TILE % WT
    k_row = k_at // span % 3 - 1
    for r in range(2):
        for j in range(3):
            q_feat[r, :, j] = q_feat[r, :, 8 + j] = q_frame == j
            q_feat[r, :, 3 + j] = q_feat[r, :, 11 + j] = q_col == j
            k_feat[r, :, j] = FAR * (abs(k_frame - j) >= 2)
            k_feat[r, :, 8 + j] = FAR * (abs(k_frame - j) == 1)
            k_feat[r, :, 3 + j] = FAR * (abs(k_col - j) >= 2)
            k_feat[r, :, 11 + j] = FAR * (abs(k_col - j) == 1)
        q_feat[r, :, 14:17] = 1.0
        k_feat[r, :, 14] = FAR * (k_row != 0)
    k_feat[0, :, 15] = FAR * (k_row == -1)
    k_feat[1, :, 16] = FAR * (k_row == 1)
    return jnp.asarray(q_feat, jnp.bfloat16), jnp.asarray(k_feat, jnp.bfloat16)


def kernel(
    n_t, n_s, frames, q_hbm, k_hbm, v_hbm, w_hbm, res_hbm, qf_hbm, kf_hbm, gate_hbm, ext_hbm,
    out, own, halo, gat, wbuf, res, acc, qf, kf, gate_ref, ext_ref,
    a_send, a_recv, a_loc, h_send, h_recv, g_send, g_recv, w_sem, c_sem,
):
    rows = q_hbm.shape[0]
    inner_dev = q_hbm.shape[1] // n_t
    heads = inner_dev // HEAD_DIM
    last = heads - 1
    span = WT * TILE
    me, sb = lax.axis_index("tensor"), lax.axis_index("seq")
    mate = me // 2 * 2 + 1 - lax.rem(me, 2)
    across = lax.rem(me + n_t // 2, n_t)
    near, far = me // 2 * 2, n_t // 2 - me // 2 * 2
    srcs = (k_hbm, v_hbm, q_hbm)
    has_up, has_down = sb < n_s - 1, sb > 0

    barrier = pltpu.get_barrier_semaphore()
    for d in range(1, n_t):
        pl.semaphore_signal(
            barrier, inc=1, device_id={"tensor": lax.rem(me + d, n_t)}, device_id_type=MESH
        )

    @pl.when(has_up)
    def _():
        pl.semaphore_signal(barrier, inc=1, device_id={"seq": sb + 1}, device_id_type=MESH)

    @pl.when(has_down)
    def _():
        pl.semaphore_signal(barrier, inc=1, device_id={"seq": sb - 1}, device_id_type=MESH)

    inner_block = has_up & has_down

    @pl.when(inner_block)
    def _():
        pl.semaphore_wait(barrier, n_t + 1)

    @pl.when(jnp.logical_not(inner_block))
    def _():
        pl.semaphore_wait(barrier, n_t)

    def columns(owner, h):
        return pl.ds(pl.multiple_of(owner * inner_dev + h * HEAD_DIM, HEAD_DIM), HEAD_DIM)

    def slot(owner):
        return pl.ds(pl.multiple_of(owner * rows, 16), rows)

    def sent(a, h, d, owner):
        peer = lax.rem(me + d, n_t)
        return pltpu.make_async_remote_copy(
            src_ref=srcs[a].at[:, columns(peer, h)],
            dst_ref=own.at[a, h, slot(owner), :],
            send_sem=a_send.at[a, h, d - 1],
            recv_sem=a_recv.at[a, h, d - 1],
            device_id={"tensor": peer},
            device_id_type=MESH,
        )

    def kept(a, h):
        return pltpu.make_async_copy(
            srcs[a].at[:, columns(me, h)], own.at[a, h, slot(me), :], a_loc.at[a, h]
        )

    def send_head(h):
        for a in range(3):
            for d in (2, 3, 1):
                sent(a, h, d, me).start()
            kept(a, h).start()

    def arrived(a, h):
        for d in range(1, n_t):
            sent(a, h, d, lax.rem(me - d + n_t, n_t)).wait_recv()
        kept(a, h).wait()

    def beside(way):
        return {"seq": sb + 1 if way == 0 else sb - 1}

    def edge(way, a, h, f):
        first = f * 2 * span + (span if way == 0 else 0)
        return pltpu.make_async_remote_copy(
            src_ref=own.at[a, h, pl.ds(first, span), :],
            dst_ref=halo.at[way, h, a, pl.ds(f * span, span), :],
            send_sem=h_send.at[way, h],
            recv_sem=h_recv.at[way, h],
            device_id=beside(way),
            device_id_type=MESH,
        )

    def edges(way, h):
        return pltpu.make_async_remote_copy(
            src_ref=halo.at[way, h],
            dst_ref=halo.at[way, h],
            send_sem=h_send.at[way, h],
            recv_sem=h_recv.at[way, h],
            device_id=beside(way),
            device_id_type=MESH,
        )

    def halo_start(h):
        for a in range(2):
            arrived(a, h)
            for way, there in ((0, has_up), (1, has_down)):

                @pl.when(there)
                def _():
                    for f in range(frames):
                        edge(way, a, h, f).start()

    def shared(h, kind, piece, part=None):
        ref = gat.at[h, piece] if part is None else gat.at[h, piece, pl.ds(part * rows, rows), :]
        at = h if part is None else last + part
        return pltpu.make_async_remote_copy(
            src_ref=ref,
            dst_ref=ref,
            send_sem=g_send.at[kind, at],
            recv_sem=g_recv.at[kind, at],
            device_id={"tensor": across if kind == 1 else mate},
            device_id_type=MESH,
        )

    diagonal = lax.rem(mate + n_t // 2, n_t)

    def weights_in(h):
        return pltpu.make_async_copy(w_hbm.at[:, h], wbuf.at[h], w_sem.at[h])

    for h in range(2):
        send_head(h)
    consts = [
        pltpu.make_async_copy(src, dst, c_sem.at[i])
        for i, (src, dst) in enumerate(
            ((qf_hbm, qf), (kf_hbm, kf), (ext_hbm, ext_ref), (gate_hbm, gate_ref), (res_hbm, res))
        )
    ]
    for copy in consts[:3]:
        copy.start()

    @pl.when(sb == 0)
    def _():
        halo[0] = jnp.zeros(halo.shape[1:], halo.dtype)

    @pl.when(sb == n_s - 1)
    def _():
        halo[1] = jnp.zeros(halo.shape[1:], halo.dtype)

    halo_start(0)

    @pl.loop(2, heads)
    def _(h):
        send_head(h)

    @pl.loop(0, heads)
    def _(h):
        weights_in(h).start()

    for copy in consts[3:]:
        copy.start()

    @pl.loop(1, AHEAD)
    def _(h):
        halo_start(h)

    acc[...] = jnp.zeros_like(acc)
    for copy in consts[:3]:
        copy.wait()

    def gathered(a, h, r):
        parts = []
        for f in range(frames):
            here = own[a, h, f * 2 * span : (f + 1) * 2 * span]
            there = halo[r, h, a, f * span : (f + 1) * span]
            parts += [there, here] if r == 0 else [here, there]
        return jnp.concatenate(parts, axis=0)

    def switches(head):
        lane = lax.broadcasted_iota(jnp.int32, (1, HEAD_DIM), 1)
        at = me * heads + head
        coef = jnp.where(lane < 8, 1.0, 0.0)
        for d, first, end in ((0, 8, 11), (2, 11, 14), (1, 14, 15)):
            stop = (1 - ext_ref[d, at]).astype(jnp.float32)
            coef = jnp.where((lane >= first) & (lane < end), stop, coef)
        coef = jnp.where(lane == 15, jnp.where(sb == 0, 1.0, 0.0), coef)
        return jnp.where(lane == 16, jnp.where(sb == n_s - 1, 1.0, 0.0), coef)

    def attend(h):
        arrived(2, h)

        @pl.when(has_down)
        def _():
            edges(0, h).wait_recv()

        @pl.when(has_up)
        def _():
            edges(1, h).wait_recv()

        ones = jnp.ones((frames * 3 * span, HEAD_DIM), jnp.bfloat16)
        coef = switches(h)
        for r in range(2):
            q_part = jnp.concatenate(
                [own[2, h, (2 * f + r) * span : (2 * f + r + 1) * span] for f in range(frames)],
                axis=0,
            )
            q_feat = (qf[r].astype(jnp.float32) * coef).astype(jnp.bfloat16)
            scores = lax.dot_general(
                jnp.concatenate([q_part, q_feat], axis=1),
                jnp.concatenate([gathered(0, h, r), kf[r]], axis=1),
                (((1,), (1,)), ((), ())),
                preferred_element_type=jnp.float32,
            )
            top = jnp.max(scores, axis=-1, keepdims=True)
            weights = jnp.exp2(
                (scores - top) * (math.log2(math.e) / math.sqrt(HEAD_DIM))
            ).astype(jnp.bfloat16)
            both = jnp.dot(
                weights,
                jnp.concatenate([gathered(1, h, r), ones], axis=1),
                preferred_element_type=jnp.float32,
            )
            done = (both[:, :HEAD_DIM] / both[:, HEAD_DIM:]).astype(jnp.bfloat16)
            for f in range(frames):
                gat[h, me, (2 * f + r) * span : (2 * f + r + 1) * span] = done[
                    f * span : (f + 1) * span
                ]

    def forward(h, part=None):
        shared(h, 1, across, part).wait_recv()
        shared(h, 2, across, part).start()

    def product(h, base, at, cols):
        lhs = jnp.concatenate([gat[h, base, at], gat[h, base + 1, at]], axis=1)
        rhs = jnp.concatenate([wbuf[h, base, :, cols], wbuf[h, base + 1, :, cols]], axis=0)
        return acc[at, cols] + jnp.dot(lhs, rhs, preferred_element_type=jnp.float32)

    def accumulate(h, base):
        @pl.loop(0, acc.shape[1] // OUT_TILE)
        def _(j):
            cols = pl.ds(pl.multiple_of(j * OUT_TILE, OUT_TILE), OUT_TILE)
            acc[:, cols] = product(h, base, slice(None), cols)

    def local(h):
        @pl.when(h == 0)
        def _():
            @pl.loop(0, heads)
            def _(i):
                weights_in(i).wait()

        shared(h, 0, mate).wait_recv()
        accumulate(h, near)

    def remote(h):
        shared(h, 2, diagonal).wait_recv()
        accumulate(h, far)

    @pl.loop(0, heads)
    def _(s):
        @pl.when(s + AHEAD < heads)
        def _():
            halo_start(s + AHEAD)

        @pl.when(s > 0)
        def _():
            local(s - 1)

        @pl.when(s == last)
        def _():
            @pl.loop(0, EARLY)
            def _(h):
                forward(h)

                @pl.when(h > 0)
                def _():
                    remote(h - 1)

        attend(s)

        @pl.when(s < last)
        def _():
            shared(s, 1, me).start()

        @pl.when(s == last)
        def _():
            for part in range(n_t):
                shared(last, 1, me, part).start()

        shared(s, 0, me).start()

    @pl.loop(EARLY, last)
    def _(h):
        forward(h)
        remote(h - 1)

        @pl.when(h == EARLY)
        def _():
            local(last)

    for copy in consts[3:]:
        copy.wait()

    def finish(part):
        shared(last, 2, diagonal, part).wait_recv()
        at = slice(part * rows, (part + 1) * rows)
        for j in range(acc.shape[1] // OUT_TILE):
            cols = slice(j * OUT_TILE, (j + 1) * OUT_TILE)
            gate = gate_ref[cols].reshape(1, OUT_TILE)
            total = product(last, far, at, cols)
            out[at, cols] = (res[at, cols].astype(jnp.float32) + gate * total).astype(out.dtype)

    forward(last, 0)
    remote(last - 1)
    for part in range(1, n_t):
        forward(last, part)
        finish(part - 1)
    finish(n_t - 1)

    @pl.loop(0, heads)
    def _(h):
        for a in range(3):
            for d in range(1, n_t):
                sent(a, h, d, me).wait_send()

        @pl.when(has_up)
        def _():
            edges(0, h).wait_send()

        @pl.when(has_down)
        def _():
            edges(1, h).wait_send()

        shared(h, 0, me).wait_send()

        @pl.when(h < last)
        def _():
            shared(h, 1, me).wait_send()
            shared(h, 2, across).wait_send()

    for part in range(n_t):
        shared(last, 1, me, part).wait_send()
        shared(last, 2, across, part).wait_send()


def shards(residual, queries, key_rows, value_rows, w_out, out_gate, extents):
    n_t, n_s = lax.axis_size("tensor"), lax.axis_size("seq")
    rows, inner = queries.shape
    tokens, out_cols = residual.shape
    inner_dev = inner // n_t
    heads = inner_dev // HEAD_DIM
    if n_t != 4 or n_s < 2 or rows % 16 or inner_dev % HEAD_DIM or heads < EARLY + 2 or out_cols % OUT_TILE:
        return plain_shards(
            residual, queries, key_rows, value_rows, w_out, out_gate, extents
        )
    frames = tokens // (HT_DEV * WT * TILE)
    half = tokens // HT_DEV
    q_feat, k_feat = mask_features(frames)
    dma = pltpu.SemaphoreType.DMA
    bf16 = jnp.bfloat16
    operands = (
        queries, key_rows, value_rows, w_out.reshape(n_t, heads, HEAD_DIM, out_cols), residual,
        q_feat, k_feat, out_gate, extents.T,
    )
    return pl.pallas_call(
        functools.partial(kernel, n_t, n_s, frames),
        out_shape=pltpu.VMEM((tokens, out_cols), bf16),
        in_specs=[pl.BlockSpec(memory_space=pl.ANY)] * len(operands),
        out_specs=pl.BlockSpec(memory_space=pltpu.VMEM),
        scratch_shapes=[
            pltpu.VMEM((3, heads, tokens, HEAD_DIM), bf16),
            pltpu.VMEM((2, heads, 2, half, HEAD_DIM), bf16),
            pltpu.VMEM((heads, n_t, tokens, HEAD_DIM), bf16),
            pltpu.VMEM((heads, n_t, HEAD_DIM, out_cols), bf16),
            pltpu.VMEM((tokens, out_cols), bf16),
            pltpu.VMEM((tokens, out_cols), jnp.float32),
            pltpu.VMEM(q_feat.shape, bf16),
            pltpu.VMEM(k_feat.shape, bf16),
            pltpu.VMEM(out_gate.shape, jnp.float32),
            pltpu.SMEM(extents.T.shape, jnp.int32),
            dma((3, heads, n_t - 1)),
            dma((3, heads, n_t - 1)),
            dma((3, heads)),
            dma((2, heads)),
            dma((2, heads)),
            dma((3, heads - 1 + n_t)),
            dma((3, heads - 1 + n_t)),
            dma((heads,)),
            dma((5,)),
        ],
        compiler_params=pltpu.CompilerParams(
            collective_id=0, has_side_effects=True, vmem_limit_bytes=40 << 20
        ),
    )(*[pltpu.with_memory_space_constraint(x, pltpu.HBM) for x in operands])


def solution(mesh):
    placed = (
        P("seq", "tensor"),
        P(("seq", "tensor"), None),
        P(("seq", "tensor"), None),
        P(("seq", "tensor"), None),
        P(None, "tensor"),
        P("tensor"),
        P(),
    )
    return jax.shard_map(
        shards, mesh=mesh, in_specs=placed, out_specs=P("seq", "tensor"), check_vma=False
    )
```

```python
import functools
import math

import jax
import jax.numpy as jnp
import numpy as np
from jax import lax
from jax.experimental import pallas as pl
from jax.experimental.pallas import tpu as pltpu
from jax.sharding import PartitionSpec as P

HEAD_DIM = 128
TILE = 32
HT_DEV = 2
WT = 3
EARLY = 4
AHEAD = 3
PARTS = 2
OUT_TILE = 512
FAR = -1e30
MESH = pl.DeviceIdType.MESH


def passed_along(value, axis, by):
    length = lax.axis_size(axis)
    pairs = [(i, i + by) for i in range(length) if 0 <= i + by < length]
    return lax.ppermute(value, axis, pairs)


def tile_coords(row_count, tile_rows, first_row):
    position = jnp.arange(row_count, dtype=jnp.int32)
    frame_id = position // (tile_rows * WT * TILE)
    row_id = first_row + position // (WT * TILE) % tile_rows
    col_id = position // TILE % WT
    return (frame_id, row_id, col_id)


def allowed_keys(query_place, key_place, head_reach, seq_block, seq_count):
    frame_gap = jnp.abs(query_place[0][:, None] - key_place[0][None, :])
    row_gap = jnp.abs(query_place[1][:, None] - key_place[1][None, :])
    col_gap = jnp.abs(query_place[2][:, None] - key_place[2][None, :])
    global_row = key_place[1] + seq_block * HT_DEV
    inside = (global_row >= 0) & (global_row < seq_count * HT_DEV)
    return (
        (frame_gap[None] <= head_reach[:, 0, None, None])
        & (row_gap[None] <= head_reach[:, 1, None, None])
        & (col_gap[None] <= head_reach[:, 2, None, None])
        & inside[None, None, :]
    )


def plain_shards(residual, queries, key_rows, value_rows, w_out, out_gate, extents):
    head_q, head_k, head_v = (
        lax.all_to_all(queries, "tensor", split_axis=1, concat_axis=0, tiled=True),
        lax.all_to_all(key_rows, "tensor", split_axis=1, concat_axis=0, tiled=True),
        lax.all_to_all(value_rows, "tensor", split_axis=1, concat_axis=0, tiled=True),
    )
    tokens, inner_dev = head_q.shape
    heads_here = inner_dev // HEAD_DIM
    seq_block = lax.axis_index("seq")
    seq_count = lax.axis_size("seq")
    head_reach = lax.dynamic_slice_in_dim(
        extents, lax.axis_index("tensor") * heads_here, heads_here, 0
    )
    query_tiles = head_q.reshape(tokens, heads_here, HEAD_DIM)
    query_place = tile_coords(tokens, HT_DEV, 0)
    stacked = jnp.stack([head_k, head_v])

    def part_scores(pair_rows, key_place):
        key_tiles = pair_rows[0].reshape(-1, heads_here, HEAD_DIM)
        scores = jnp.einsum(
            "qhd,khd->hqk", query_tiles, key_tiles, preferred_element_type=jnp.float32
        ) / math.sqrt(HEAD_DIM)
        allowed = allowed_keys(query_place, key_place, head_reach, seq_block, seq_count)
        return jnp.where(allowed, scores, FAR)

    by_row = stacked.reshape(2, -1, HT_DEV, WT * TILE, inner_dev)
    halves = tokens // HT_DEV
    last_row = by_row[:, :, HT_DEV - 1].reshape(2, halves, inner_dev)
    first_row = by_row[:, :, 0].reshape(2, halves, inner_dev)
    parts = [
        (stacked, query_place),
        (passed_along(last_row, "seq", 1), tile_coords(halves, 1, -1)),
        (passed_along(first_row, "seq", -1), tile_coords(halves, 1, HT_DEV)),
    ]
    scores = jnp.concatenate([part_scores(*part) for part in parts], axis=-1)
    value_all = jnp.concatenate([pair_rows[1] for pair_rows, _ in parts], axis=0)
    row_max = jnp.max(scores, axis=-1, keepdims=True)
    exp_scores = jnp.exp(scores - row_max)
    row_sum = jnp.sum(exp_scores, axis=-1, keepdims=True)
    weights = (exp_scores / row_sum).astype(jnp.bfloat16)
    attended = jnp.einsum(
        "hqk,khd->qhd",
        weights,
        value_all.reshape(-1, heads_here, HEAD_DIM),
        preferred_element_type=jnp.float32,
    )
    head_out = attended.reshape(tokens, inner_dev).astype(jnp.bfloat16)
    projected = jnp.dot(
        lax.all_gather(head_out, "tensor", axis=1, tiled=True),
        w_out,
        preferred_element_type=jnp.float32,
    )
    return (residual.astype(jnp.float32) + out_gate * projected).astype(jnp.bfloat16)


def mask_features(frames):
    span = WT * TILE
    q_feat = np.zeros((2, frames * span, HEAD_DIM), np.float32)
    k_feat = np.zeros((2, frames * 3 * span, HEAD_DIM), np.float32)
    q_at = np.arange(frames * span)
    q_frame, q_col = q_at // span, q_at // TILE % WT
    k_at = np.arange(frames * 3 * span)
    k_frame, k_col = k_at // (3 * span), k_at // TILE % WT
    k_row = k_at // span % 3 - 1
    for r in range(2):
        for j in range(3):
            q_feat[r, :, j] = q_feat[r, :, 8 + j] = q_frame == j
            q_feat[r, :, 3 + j] = q_feat[r, :, 11 + j] = q_col == j
            k_feat[r, :, j] = FAR * (abs(k_frame - j) >= 2)
            k_feat[r, :, 8 + j] = FAR * (abs(k_frame - j) == 1)
            k_feat[r, :, 3 + j] = FAR * (abs(k_col - j) >= 2)
            k_feat[r, :, 11 + j] = FAR * (abs(k_col - j) == 1)
        q_feat[r, :, 14:17] = 1.0
        k_feat[r, :, 14] = FAR * (k_row != 0)
    k_feat[0, :, 15] = FAR * (k_row == -1)
    k_feat[1, :, 16] = FAR * (k_row == 1)
    return jnp.asarray(q_feat, jnp.bfloat16), jnp.asarray(k_feat, jnp.bfloat16)


def kernel(
    n_t, n_s, frames, q_hbm, k_hbm, v_hbm, w_hbm, res_hbm, qf_hbm, kf_hbm, gate_hbm, ext_hbm,
    out, own, halo, gat, wbuf, res, acc, qf, kf, gate_ref, ext_ref,
    a_send, a_recv, a_loc, h_send, h_recv, g_send, g_recv, w_sem, c_sem,
):
    rows = q_hbm.shape[0]
    inner_dev = q_hbm.shape[1] // n_t
    heads = inner_dev // HEAD_DIM
    last = heads - 1
    piece_rows = n_t * rows // PARTS
    span = WT * TILE
    me, sb = lax.axis_index("tensor"), lax.axis_index("seq")
    mate = me // 2 * 2 + 1 - lax.rem(me, 2)
    across = lax.rem(me + n_t // 2, n_t)
    near, far = me // 2 * 2, n_t // 2 - me // 2 * 2
    srcs = (k_hbm, v_hbm, q_hbm)
    has_up, has_down = sb < n_s - 1, sb > 0

    barrier = pltpu.get_barrier_semaphore()
    for d in range(1, n_t):
        pl.semaphore_signal(
            barrier, inc=1, device_id={"tensor": lax.rem(me + d, n_t)}, device_id_type=MESH
        )

    @pl.when(has_up)
    def _():
        pl.semaphore_signal(barrier, inc=1, device_id={"seq": sb + 1}, device_id_type=MESH)

    @pl.when(has_down)
    def _():
        pl.semaphore_signal(barrier, inc=1, device_id={"seq": sb - 1}, device_id_type=MESH)

    inner_block = has_up & has_down

    @pl.when(inner_block)
    def _():
        pl.semaphore_wait(barrier, n_t + 1)

    @pl.when(jnp.logical_not(inner_block))
    def _():
        pl.semaphore_wait(barrier, n_t)

    def columns(owner, h):
        return pl.ds(pl.multiple_of(owner * inner_dev + h * HEAD_DIM, HEAD_DIM), HEAD_DIM)

    def slot(owner):
        return pl.ds(pl.multiple_of(owner * rows, 16), rows)

    def sent(a, h, d, owner):
        peer = lax.rem(me + d, n_t)
        return pltpu.make_async_remote_copy(
            src_ref=srcs[a].at[:, columns(peer, h)],
            dst_ref=own.at[a, h, slot(owner), :],
            send_sem=a_send.at[h],
            recv_sem=a_recv.at[a, h],
            device_id={"tensor": peer},
            device_id_type=MESH,
        )

    def kept(a, h):
        return pltpu.make_async_copy(
            srcs[a].at[:, columns(me, h)], own.at[a, h, slot(me), :], a_loc.at[a, h]
        )

    def send_head(h):
        for a in range(3):
            for d in (2, 3, 1):
                sent(a, h, d, me).start()
            kept(a, h).start()

    def whole(ref, h, at):
        return pltpu.make_async_remote_copy(
            src_ref=ref,
            dst_ref=ref,
            send_sem=a_send.at[h],
            recv_sem=a_recv.at[at, h],
            device_id={"tensor": mate},
            device_id_type=MESH,
        )

    others = pl.ds(0, (n_t - 1) * rows)

    def arrived(a, h):
        whole(own.at[a, h, others, :], h, a).wait_recv()
        kept(a, h).wait()

    def beside(way):
        return {"seq": sb + 1 if way == 0 else sb - 1}

    def edge(way, a, h, f):
        first = f * 2 * span + (span if way == 0 else 0)
        return pltpu.make_async_remote_copy(
            src_ref=own.at[a, h, pl.ds(first, span), :],
            dst_ref=halo.at[way, h, a, pl.ds(f * span, span), :],
            send_sem=h_send.at[way, h],
            recv_sem=h_recv.at[way, h],
            device_id=beside(way),
            device_id_type=MESH,
        )

    def edges(way, h):
        return pltpu.make_async_remote_copy(
            src_ref=halo.at[way, h],
            dst_ref=halo.at[way, h],
            send_sem=h_send.at[way, h],
            recv_sem=h_recv.at[way, h],
            device_id=beside(way),
            device_id_type=MESH,
        )

    def edges_out(h):
        @pl.when(has_up)
        def _():
            edges(0, h).wait_send()

        @pl.when(has_down)
        def _():
            edges(1, h).wait_send()

    def halo_start(h):
        for a in range(2):
            arrived(a, h)
            for way, there in ((0, has_up), (1, has_down)):

                @pl.when(there)
                def _():
                    for f in range(frames):
                        edge(way, a, h, f).start()

    def shared(h, kind, piece, part=None):
        ref = gat.at[h, piece] if part is None else gat.at[h, piece, pl.ds(part * piece_rows, piece_rows), :]
        at = h if part is None else last + part
        return pltpu.make_async_remote_copy(
            src_ref=ref,
            dst_ref=ref,
            send_sem=g_send.at[kind, at],
            recv_sem=g_recv.at[kind, at],
            device_id={"tensor": across if kind == 1 else mate},
            device_id_type=MESH,
        )

    diagonal = lax.rem(mate + n_t // 2, n_t)

    def weights_in(h):
        return pltpu.make_async_copy(w_hbm.at[:, h], wbuf.at[h], w_sem.at[h])

    for h in range(2):
        send_head(h)
    consts = [
        pltpu.make_async_copy(src, dst, c_sem.at[i])
        for i, (src, dst) in enumerate(
            ((qf_hbm, qf), (kf_hbm, kf), (ext_hbm, ext_ref), (gate_hbm, gate_ref), (res_hbm, res))
        )
    ]
    for copy in consts[:3]:
        copy.start()

    @pl.when(sb == 0)
    def _():
        halo[0] = jnp.zeros(halo.shape[1:], halo.dtype)

    @pl.when(sb == n_s - 1)
    def _():
        halo[1] = jnp.zeros(halo.shape[1:], halo.dtype)

    halo_start(0)

    @pl.loop(2, heads)
    def _(h):
        send_head(h)

    @pl.loop(0, heads)
    def _(h):
        weights_in(h).start()

    for copy in consts[3:]:
        copy.start()

    @pl.loop(1, AHEAD)
    def _(h):
        halo_start(h)

    acc[...] = jnp.zeros_like(acc)
    for copy in consts[:3]:
        copy.wait()

    def gathered(a, h, r):
        parts = []
        for f in range(frames):
            here = own[a, h, f * 2 * span : (f + 1) * 2 * span]
            there = halo[r, h, a, f * span : (f + 1) * span]
            parts += [there, here] if r == 0 else [here, there]
        return jnp.concatenate(parts, axis=0)

    def switches(head):
        lane = lax.broadcasted_iota(jnp.int32, (1, HEAD_DIM), 1)
        at = me * heads + head
        coef = jnp.where(lane < 8, 1.0, 0.0)
        for d, first, end in ((0, 8, 11), (2, 11, 14), (1, 14, 15)):
            stop = (1 - ext_ref[d, at]).astype(jnp.float32)
            coef = jnp.where((lane >= first) & (lane < end), stop, coef)
        coef = jnp.where(lane == 15, jnp.where(sb == 0, 1.0, 0.0), coef)
        return jnp.where(lane == 16, jnp.where(sb == n_s - 1, 1.0, 0.0), coef)

    def attend(h):
        arrived(2, h)

        @pl.when(has_down)
        def _():
            edges(0, h).wait_recv()

        @pl.when(has_up)
        def _():
            edges(1, h).wait_recv()

        ones = jnp.ones((frames * 3 * span, HEAD_DIM), jnp.bfloat16)
        coef = switches(h)
        for r in range(2):
            q_part = jnp.concatenate(
                [own[2, h, (2 * f + r) * span : (2 * f + r + 1) * span] for f in range(frames)],
                axis=0,
            )
            q_feat = (qf[r].astype(jnp.float32) * coef).astype(jnp.bfloat16)
            scores = lax.dot_general(
                jnp.concatenate([q_part, q_feat], axis=1),
                jnp.concatenate([gathered(0, h, r), kf[r]], axis=1),
                (((1,), (1,)), ((), ())),
                preferred_element_type=jnp.float32,
            )
            top = jnp.max(scores, axis=-1, keepdims=True)
            weights = jnp.exp2(
                (scores - top) * (math.log2(math.e) / math.sqrt(HEAD_DIM))
            ).astype(jnp.bfloat16)
            both = jnp.dot(
                weights,
                jnp.concatenate([gathered(1, h, r), ones], axis=1),
                preferred_element_type=jnp.float32,
            )
            done = (both[:, :HEAD_DIM] / both[:, HEAD_DIM:]).astype(jnp.bfloat16)
            for f in range(frames):
                gat[h, me, (2 * f + r) * span : (2 * f + r + 1) * span] = done[
                    f * span : (f + 1) * span
                ]

    def forward(h, part=None):
        shared(h, 1, across, part).wait_recv()
        shared(h, 2, across, part).start()

    def product(h, base, at, cols):
        pieces = [(h + i, base + j) for i in range(2) for j in range(2)]
        lhs = jnp.concatenate([gat[i, j, at] for i, j in pieces], axis=1)
        rhs = jnp.concatenate([wbuf[i, j, :, cols] for i, j in pieces], axis=0)
        return acc[at, cols] + jnp.dot(lhs, rhs, preferred_element_type=jnp.float32)

    def accumulate(h, base):
        @pl.loop(0, acc.shape[1] // OUT_TILE)
        def _(j):
            cols = pl.ds(pl.multiple_of(j * OUT_TILE, OUT_TILE), OUT_TILE)
            acc[:, cols] = product(h, base, slice(None), cols)

    def local(h):
        shared(h, 0, mate).wait_recv()
        shared(h + 1, 0, mate).wait_recv()
        accumulate(h, near)

    def remote(h):
        shared(h, 2, diagonal).wait_recv()
        shared(h + 1, 2, diagonal).wait_recv()
        accumulate(h, far)

    @pl.loop(0, heads)
    def _(s):
        @pl.when(s + AHEAD < heads)
        def _():
            halo_start(s + AHEAD)

        @pl.when(s == 2)
        def _():
            @pl.loop(0, heads)
            def _(i):
                weights_in(i).wait()

        @pl.when((s > 0) & (lax.rem(s, 2) == 0))
        def _():
            local(s - 2)

        @pl.when(s == last)
        def _():
            @pl.loop(0, EARLY)
            def _(h):
                forward(h)

                @pl.when((h > 0) & (lax.rem(h, 2) == 0))
                def _():
                    remote(h - 2)

        @pl.when(s > 0)
        def _():
            whole(own.at[:, s - 1, others, :], s - 1, 0).wait_send()
            shared(s - 1, 0, me).wait_send()

        @pl.when(s > 1)
        def _():
            edges_out(s - 2)

        attend(s)

        @pl.when(s < last)
        def _():
            shared(s, 1, me).start()

        @pl.when(s == last)
        def _():
            for part in range(PARTS):
                shared(last, 1, me, part).start()

        shared(s, 0, me).start()

    @pl.loop(EARLY, last)
    def _(h):
        forward(h)

        @pl.when(lax.rem(h, 2) == 0)
        def _():
            remote(h - 2)

        @pl.when(h == EARLY)
        def _():
            local(last - 1)

    for copy in consts[3:]:
        copy.wait()

    def finish(part):
        shared(last, 2, diagonal, part).wait_recv()
        at = slice(part * piece_rows, (part + 1) * piece_rows)
        for j in range(acc.shape[1] // OUT_TILE):
            cols = slice(j * OUT_TILE, (j + 1) * OUT_TILE)
            gate = gate_ref[cols].reshape(1, OUT_TILE)
            total = product(last - 1, far, at, cols)
            out[at, cols] = (res[at, cols].astype(jnp.float32) + gate * total).astype(out.dtype)

    whole(own.at[:, last, others, :], last, 0).wait_send()
    shared(last, 0, me).wait_send()
    for h in (last - 1, last):
        edges_out(h)

    @pl.loop(0, last)
    def _(h):
        shared(h, 1, me).wait_send()

        @pl.when(h < last - 1)
        def _():
            shared(h, 2, across).wait_send()

    forward(last, 0)
    shared(last - 1, 2, across).wait_send()
    shared(last - 1, 2, diagonal).wait_recv()
    for part in range(1, PARTS):
        forward(last, part)
        finish(part - 1)
    finish(PARTS - 1)

    for part in range(PARTS):
        shared(last, 1, me, part).wait_send()
        shared(last, 2, across, part).wait_send()


def shards(residual, queries, key_rows, value_rows, w_out, out_gate, extents):
    n_t, n_s = lax.axis_size("tensor"), lax.axis_size("seq")
    rows, inner = queries.shape
    tokens, out_cols = residual.shape
    inner_dev = inner // n_t
    heads = inner_dev // HEAD_DIM
    if n_t != 4 or n_s < 2 or rows % 16 or inner_dev % HEAD_DIM or heads < EARLY + 2 or heads % 2 or rows % (4 * PARTS) or out_cols % OUT_TILE:
        return plain_shards(
            residual, queries, key_rows, value_rows, w_out, out_gate, extents
        )
    frames = tokens // (HT_DEV * WT * TILE)
    half = tokens // HT_DEV
    q_feat, k_feat = mask_features(frames)
    dma = pltpu.SemaphoreType.DMA
    bf16 = jnp.bfloat16
    operands = (
        queries, key_rows, value_rows, w_out.reshape(n_t, heads, HEAD_DIM, out_cols), residual,
        q_feat, k_feat, out_gate, extents.T,
    )
    return pl.pallas_call(
        functools.partial(kernel, n_t, n_s, frames),
        out_shape=pltpu.VMEM((tokens, out_cols), bf16),
        in_specs=[pl.BlockSpec(memory_space=pl.ANY)] * len(operands),
        out_specs=pl.BlockSpec(memory_space=pltpu.VMEM),
        scratch_shapes=[
            pltpu.VMEM((3, heads, tokens, HEAD_DIM), bf16),
            pltpu.VMEM((2, heads, 2, half, HEAD_DIM), bf16),
            pltpu.VMEM((heads, n_t, tokens, HEAD_DIM), bf16),
            pltpu.VMEM((heads, n_t, HEAD_DIM, out_cols), bf16),
            pltpu.VMEM((tokens, out_cols), bf16),
            pltpu.VMEM((tokens, out_cols), jnp.float32),
            pltpu.VMEM(q_feat.shape, bf16),
            pltpu.VMEM(k_feat.shape, bf16),
            pltpu.VMEM(out_gate.shape, jnp.float32),
            pltpu.SMEM(extents.T.shape, jnp.int32),
            dma((heads,)),
            dma((3, heads)),
            dma((3, heads)),
            dma((2, heads)),
            dma((2, heads)),
            dma((3, heads - 1 + PARTS)),
            dma((3, heads - 1 + PARTS)),
            dma((heads,)),
            dma((5,)),
        ],
        compiler_params=pltpu.CompilerParams(
            collective_id=0, has_side_effects=True, vmem_limit_bytes=40 << 20
        ),
    )(*[pltpu.with_memory_space_constraint(x, pltpu.HBM) for x in operands])


def solution(mesh):
    placed = (
        P("seq", "tensor"),
        P(("seq", "tensor"), None),
        P(("seq", "tensor"), None),
        P(("seq", "tensor"), None),
        P(None, "tensor"),
        P("tensor"),
        P(),
    )
    return jax.shard_map(
        shards, mesh=mesh, in_specs=placed, out_specs=P("seq", "tensor"), check_vma=False
    )
```

```python
import functools
import math

import jax
import jax.numpy as jnp
import numpy as np
from jax import lax
from jax.experimental import pallas as pl
from jax.experimental.pallas import tpu as pltpu
from jax.sharding import PartitionSpec as P

HEAD_DIM = 128
TILE = 32
HT_DEV = 2
WT = 3
HEADS_DEV = 8
PARTS = 2
KV_GROUPS = ((0, 1), (1, 1), (2, 2), (4, 2), (6, 2))
Q_GROUPS = ((0, 2), (2, 2), (4, 4))
EDGE_GROUPS = tuple((h, 1) for h in range(HEADS_DEV))
OUT_TILE = 512
FAR = -1e30
MESH = pl.DeviceIdType.MESH


def passed_along(value, axis, by):
    length = lax.axis_size(axis)
    pairs = [(i, i + by) for i in range(length) if 0 <= i + by < length]
    return lax.ppermute(value, axis, pairs)


def tile_coords(row_count, tile_rows, first_row):
    position = jnp.arange(row_count, dtype=jnp.int32)
    frame_id = position // (tile_rows * WT * TILE)
    row_id = first_row + position // (WT * TILE) % tile_rows
    col_id = position // TILE % WT
    return (frame_id, row_id, col_id)


def allowed_keys(query_place, key_place, head_reach, seq_block, seq_count):
    frame_gap = jnp.abs(query_place[0][:, None] - key_place[0][None, :])
    row_gap = jnp.abs(query_place[1][:, None] - key_place[1][None, :])
    col_gap = jnp.abs(query_place[2][:, None] - key_place[2][None, :])
    global_row = key_place[1] + seq_block * HT_DEV
    inside = (global_row >= 0) & (global_row < seq_count * HT_DEV)
    return (
        (frame_gap[None] <= head_reach[:, 0, None, None])
        & (row_gap[None] <= head_reach[:, 1, None, None])
        & (col_gap[None] <= head_reach[:, 2, None, None])
        & inside[None, None, :]
    )


def plain_shards(residual, queries, key_rows, value_rows, w_out, out_gate, extents):
    head_q, head_k, head_v = (
        lax.all_to_all(queries, "tensor", split_axis=1, concat_axis=0, tiled=True),
        lax.all_to_all(key_rows, "tensor", split_axis=1, concat_axis=0, tiled=True),
        lax.all_to_all(value_rows, "tensor", split_axis=1, concat_axis=0, tiled=True),
    )
    tokens, inner_dev = head_q.shape
    heads_here = inner_dev // HEAD_DIM
    seq_block = lax.axis_index("seq")
    seq_count = lax.axis_size("seq")
    head_reach = lax.dynamic_slice_in_dim(
        extents, lax.axis_index("tensor") * heads_here, heads_here, 0
    )
    query_tiles = head_q.reshape(tokens, heads_here, HEAD_DIM)
    query_place = tile_coords(tokens, HT_DEV, 0)
    stacked = jnp.stack([head_k, head_v])

    def part_scores(pair_rows, key_place):
        key_tiles = pair_rows[0].reshape(-1, heads_here, HEAD_DIM)
        scores = jnp.einsum(
            "qhd,khd->hqk", query_tiles, key_tiles, preferred_element_type=jnp.float32
        ) / math.sqrt(HEAD_DIM)
        allowed = allowed_keys(query_place, key_place, head_reach, seq_block, seq_count)
        return jnp.where(allowed, scores, FAR)

    by_row = stacked.reshape(2, -1, HT_DEV, WT * TILE, inner_dev)
    halves = tokens // HT_DEV
    last_row = by_row[:, :, HT_DEV - 1].reshape(2, halves, inner_dev)
    first_row = by_row[:, :, 0].reshape(2, halves, inner_dev)
    parts = [
        (stacked, query_place),
        (passed_along(last_row, "seq", 1), tile_coords(halves, 1, -1)),
        (passed_along(first_row, "seq", -1), tile_coords(halves, 1, HT_DEV)),
    ]
    scores = jnp.concatenate([part_scores(*part) for part in parts], axis=-1)
    value_all = jnp.concatenate([pair_rows[1] for pair_rows, _ in parts], axis=0)
    row_max = jnp.max(scores, axis=-1, keepdims=True)
    exp_scores = jnp.exp(scores - row_max)
    row_sum = jnp.sum(exp_scores, axis=-1, keepdims=True)
    weights = (exp_scores / row_sum).astype(jnp.bfloat16)
    attended = jnp.einsum(
        "hqk,khd->qhd",
        weights,
        value_all.reshape(-1, heads_here, HEAD_DIM),
        preferred_element_type=jnp.float32,
    )
    head_out = attended.reshape(tokens, inner_dev).astype(jnp.bfloat16)
    projected = jnp.dot(
        lax.all_gather(head_out, "tensor", axis=1, tiled=True),
        w_out,
        preferred_element_type=jnp.float32,
    )
    return (residual.astype(jnp.float32) + out_gate * projected).astype(jnp.bfloat16)


def mask_features(frames):
    span = WT * TILE
    q_feat = np.zeros((2, frames * span, HEAD_DIM), np.float32)
    k_feat = np.zeros((2, frames * 3 * span, HEAD_DIM), np.float32)
    q_at = np.arange(frames * span)
    q_frame, q_col = q_at // span, q_at // TILE % WT
    k_at = np.arange(frames * 3 * span)
    k_frame, k_col = k_at // (3 * span), k_at // TILE % WT
    k_row = k_at // span % 3 - 1
    for r in range(2):
        for j in range(3):
            q_feat[r, :, j] = q_feat[r, :, 8 + j] = q_frame == j
            q_feat[r, :, 3 + j] = q_feat[r, :, 11 + j] = q_col == j
            k_feat[r, :, j] = FAR * (abs(k_frame - j) >= 2)
            k_feat[r, :, 8 + j] = FAR * (abs(k_frame - j) == 1)
            k_feat[r, :, 3 + j] = FAR * (abs(k_col - j) >= 2)
            k_feat[r, :, 11 + j] = FAR * (abs(k_col - j) == 1)
        q_feat[r, :, 14:17] = 1.0
        k_feat[r, :, 14] = FAR * (k_row != 0)
    k_feat[0, :, 15] = FAR * (k_row == -1)
    k_feat[1, :, 16] = FAR * (k_row == 1)
    return jnp.asarray(q_feat, jnp.bfloat16), jnp.asarray(k_feat, jnp.bfloat16)


def kernel(
    n_t, n_s, frames, q_hbm, k_hbm, v_hbm, w_hbm, res_hbm, qf_hbm, kf_hbm, gate_hbm, ext_hbm,
    out, own, halo, gat, wbuf, res, acc, qf, kf, gate_ref, ext_ref,
    a_send, a_recv, a_loc, h_send, h_recv, g_send, g_recv, w_sem, c_sem,
):
    rows = q_hbm.shape[0]
    inner_dev = q_hbm.shape[1] // n_t
    heads = inner_dev // HEAD_DIM
    last = heads - 1
    piece_rows = n_t * rows // PARTS
    span = WT * TILE
    me, sb = lax.axis_index("tensor"), lax.axis_index("seq")
    mate = me // 2 * 2 + 1 - lax.rem(me, 2)
    across = lax.rem(me + n_t // 2, n_t)
    near, far = me // 2 * 2, n_t // 2 - me // 2 * 2
    srcs = (k_hbm, v_hbm, q_hbm)
    has_up, has_down = sb < n_s - 1, sb > 0

    barrier = pltpu.get_barrier_semaphore()
    for d in range(1, n_t):
        pl.semaphore_signal(
            barrier, inc=1, device_id={"tensor": lax.rem(me + d, n_t)}, device_id_type=MESH
        )

    @pl.when(has_up)
    def _():
        pl.semaphore_signal(barrier, inc=1, device_id={"seq": sb + 1}, device_id_type=MESH)

    @pl.when(has_down)
    def _():
        pl.semaphore_signal(barrier, inc=1, device_id={"seq": sb - 1}, device_id_type=MESH)

    inner_block = has_up & has_down

    @pl.when(inner_block)
    def _():
        pl.semaphore_wait(barrier, n_t + 1)

    @pl.when(jnp.logical_not(inner_block))
    def _():
        pl.semaphore_wait(barrier, n_t)

    def columns(first, count):
        return pl.ds(pl.multiple_of(first * HEAD_DIM, HEAD_DIM), count * HEAD_DIM)

    def slot(owner):
        return pl.ds(pl.multiple_of(owner * rows, 16), rows)

    def sent(a, d, group, sem):
        first, count = group
        peer = lax.rem(me + d, n_t)
        return pltpu.make_async_remote_copy(
            src_ref=srcs[a].at[:, columns(peer * heads + first, count)],
            dst_ref=own.at[a, slot(me), columns(first, count)],
            send_sem=a_send.at[sem],
            recv_sem=a_recv.at[sem],
            device_id={"tensor": peer},
            device_id_type=MESH,
        )

    def sent_all(arrays, group, sem):
        first, count = group
        ref = own.at[arrays, pl.ds(0, (n_t - 1) * rows), columns(first, count)]
        return pltpu.make_async_remote_copy(
            src_ref=ref,
            dst_ref=ref,
            send_sem=a_send.at[sem],
            recv_sem=a_recv.at[sem],
            device_id={"tensor": mate},
            device_id_type=MESH,
        )

    kv_all = [sent_all(pl.ds(0, 2), g, i) for i, g in enumerate(KV_GROUPS)]
    q_all = [sent_all(pl.ds(2, 1), g, len(KV_GROUPS) + i) for i, g in enumerate(Q_GROUPS)]

    def send_kv(i):
        for a in range(2):
            for d in (2, 3, 1):
                sent(a, d, KV_GROUPS[i], i).start()

    def send_q(i):
        for d in (2, 3, 1):
            sent(2, d, Q_GROUPS[i], len(KV_GROUPS) + i).start()

    kept = [
        pltpu.make_async_copy(
            srcs[a].at[:, columns(me * heads, heads)], own.at[a, slot(me), :], a_loc.at[a]
        )
        for a in range(3)
    ]

    def edges(way, i):
        first, count = EDGE_GROUPS[i]
        by_frame = own.reshape(3, frames, 2 * span, inner_dev)
        return pltpu.make_async_remote_copy(
            src_ref=by_frame.at[
                pl.ds(0, 2), :, pl.ds(span if way == 0 else 0, span), columns(first, count)
            ],
            dst_ref=halo.at[way, :, :, :, columns(first, count)],
            send_sem=h_send.at[way, i],
            recv_sem=h_recv.at[way, i],
            device_id={"seq": sb + 1 if way == 0 else sb - 1},
            device_id_type=MESH,
        )

    def edges_start(i):
        @pl.when(has_up)
        def _():
            edges(0, i).start()

        @pl.when(has_down)
        def _():
            edges(1, i).start()

    def edges_in(i):
        @pl.when(has_down)
        def _():
            edges(0, i).wait_recv()

        @pl.when(has_up)
        def _():
            edges(1, i).wait_recv()

    def edges_out(i):
        @pl.when(has_up)
        def _():
            edges(0, i).wait_send()

        @pl.when(has_down)
        def _():
            edges(1, i).wait_send()

    def shared(kind, piece, first, count=1, part=None):
        if part is None:
            ref, at = gat.at[pl.ds(first, count), piece], first
        else:
            ref = gat.at[first, piece, pl.ds(part * piece_rows, piece_rows), :]
            at = first + part
        return pltpu.make_async_remote_copy(
            src_ref=ref,
            dst_ref=ref,
            send_sem=g_send.at[kind, at],
            recv_sem=g_recv.at[kind, at],
            device_id={"tensor": across if kind == 1 else mate},
            device_id_type=MESH,
        )

    diagonal = lax.rem(mate + n_t // 2, n_t)

    def weights_in(owner):
        return pltpu.make_async_copy(w_hbm.at[owner], wbuf.at[owner], w_sem.at[owner])

    send_kv(0)
    kept[0].start()
    kept[1].start()
    send_kv(1)
    send_kv(2)
    kept[2].start()
    consts = [
        pltpu.make_async_copy(src, dst, c_sem.at[i])
        for i, (src, dst) in enumerate(
            ((qf_hbm, qf), (kf_hbm, kf), (ext_hbm, ext_ref), (gate_hbm, gate_ref), (res_hbm, res))
        )
    ]

    @pl.when(sb == 0)
    def _():
        halo[0] = jnp.zeros(halo.shape[1:], halo.dtype)

    @pl.when(sb == n_s - 1)
    def _():
        halo[1] = jnp.zeros(halo.shape[1:], halo.dtype)

    kept[0].wait()
    kept[1].wait()
    kv_all[0].wait_recv()
    edges_start(0)
    send_q(0)
    send_kv(3)
    send_kv(4)
    send_q(1)
    send_q(2)
    for copy in consts:
        copy.start()
    for owner in range(n_t):
        weights_in(owner).start()
    kv_all[1].wait_recv()
    edges_start(1)
    acc[...] = jnp.zeros_like(acc)
    kv_all[2].wait_recv()
    edges_start(2)
    edges_start(3)
    for copy in consts:
        copy.wait()
    kept[2].wait()
    for owner in range(n_t):
        weights_in(owner).wait()

    def gathered(a, h, r):
        parts = []
        for f in range(frames):
            here = own[a, f * 2 * span : (f + 1) * 2 * span, columns(h, 1)]
            there = halo[r, a, f, :, columns(h, 1)]
            parts += [there, here] if r == 0 else [here, there]
        return jnp.concatenate(parts, axis=0)

    def switches(head):
        lane = lax.broadcasted_iota(jnp.int32, (1, HEAD_DIM), 1)
        at = me * heads + head
        coef = jnp.where(lane < 8, 1.0, 0.0)
        for d, first, end in ((0, 8, 11), (2, 11, 14), (1, 14, 15)):
            stop = (1 - ext_ref[d, at]).astype(jnp.float32)
            coef = jnp.where((lane >= first) & (lane < end), stop, coef)
        coef = jnp.where(lane == 15, jnp.where(sb == 0, 1.0, 0.0), coef)
        return jnp.where(lane == 16, jnp.where(sb == n_s - 1, 1.0, 0.0), coef)

    def attend(h):
        ones = jnp.ones((frames * 3 * span, HEAD_DIM), jnp.bfloat16)
        coef = switches(h)
        for r in range(2):
            q_part = jnp.concatenate(
                [
                    own[2, (2 * f + r) * span : (2 * f + r + 1) * span, columns(h, 1)]
                    for f in range(frames)
                ],
                axis=0,
            )
            q_feat = (qf[r].astype(jnp.float32) * coef).astype(jnp.bfloat16)
            scores = lax.dot_general(
                jnp.concatenate([q_part, q_feat], axis=1),
                jnp.concatenate([gathered(0, h, r), kf[r]], axis=1),
                (((1,), (1,)), ((), ())),
                preferred_element_type=jnp.float32,
            )
            top = jnp.max(scores, axis=-1, keepdims=True)
            weights = jnp.exp2(
                (scores - top) * (math.log2(math.e) / math.sqrt(HEAD_DIM))
            ).astype(jnp.bfloat16)
            both = jnp.dot(
                weights,
                jnp.concatenate([gathered(1, h, r), ones], axis=1),
                preferred_element_type=jnp.float32,
            )
            done = (both[:, :HEAD_DIM] / both[:, HEAD_DIM:]).astype(jnp.bfloat16)
            for f in range(frames):
                gat[h, me, (2 * f + r) * span : (2 * f + r + 1) * span] = done[
                    f * span : (f + 1) * span
                ]

    def forward(first, count=1, part=None):
        if part is None:
            for h in range(first, first + count):
                shared(1, across, h).wait_recv()
        else:
            shared(1, across, first, count, part).wait_recv()
        shared(2, across, first, count, part).start()

    def product(h, base, at, cols):
        pieces = [(h + i, base + j) for i in range(2) for j in range(2)]
        lhs = jnp.concatenate([gat[i, j, at] for i, j in pieces], axis=1)
        rhs = jnp.concatenate([wbuf[j, i, :, cols] for i, j in pieces], axis=0)
        return acc[at, cols] + jnp.dot(lhs, rhs, preferred_element_type=jnp.float32)

    def accumulate(h, base):
        @pl.loop(0, acc.shape[1] // OUT_TILE)
        def _(j):
            cols = pl.ds(pl.multiple_of(j * OUT_TILE, OUT_TILE), OUT_TILE)
            acc[:, cols] = product(h, base, slice(None), cols)

    def local(h):
        shared(0, mate, h, 2).wait_recv()
        accumulate(h, near)

    def remote(h):
        shared(2, diagonal, h, 2).wait_recv()
        accumulate(h, far)

    def before(s):
        if s == 2:
            local(0)
            kv_all[3].wait_recv()
            edges_start(4)
            edges_start(5)
            kv_all[4].wait_recv()
            edges_start(6)
            edges_start(7)
        if s == 4:
            local(2)
            for i in range(3):
                kv_all[i].wait_send()
        if s == 5:
            for i in range(3):
                edges_out(i)
            shared(0, me, 0, 2).wait_send()
            shared(0, me, 2, 2).wait_send()
        if s == 6:
            local(4)
            for i in range(3):
                q_all[i].wait_send()
            kv_all[3].wait_send()
            kv_all[4].wait_send()
            forward(0, 2)
        if s == 7:
            for i in range(3, 6):
                edges_out(i)
            shared(0, me, 4, 2).wait_send()
            shared(1, me, 0).wait_send()
            shared(1, me, 1).wait_send()
            remote(0)
            forward(2, 2)
            shared(2, across, 0, 2).wait_send()
        if s in (0, 2, 4):
            q_all[s // 2].wait_recv()
        for i, (first, _) in enumerate(EDGE_GROUPS):
            if first == s:
                edges_in(i)

    def after(s):
        if s < 7:
            shared(1, me, s).start()
        if s == 7:
            for part in range(PARTS):
                shared(1, me, 7, 1, part).start()
        if s % 2:
            shared(0, me, s - 1, 2).start()

    @pl.loop(0, heads)
    def _(s):
        for i in range(HEADS_DEV):
            pl.when(s == i)(functools.partial(before, i))

        attend(s)

        for i in range(HEADS_DEV):
            pl.when(s == i)(functools.partial(after, i))

    remote(2)
    forward(4, 2)
    local(6)
    shared(1, me, 2).wait_send()
    shared(1, me, 3).wait_send()
    shared(2, across, 2, 2).wait_send()
    remote(4)
    edges_out(6)
    edges_out(7)
    forward(6)
    shared(0, me, 6, 2).wait_send()
    shared(1, me, 4).wait_send()
    shared(1, me, 5).wait_send()
    shared(2, across, 4, 2).wait_send()

    def finish(part):
        shared(2, diagonal, 7, 1, part).wait_recv()
        at = slice(part * piece_rows, (part + 1) * piece_rows)
        for j in range(acc.shape[1] // OUT_TILE):
            cols = slice(j * OUT_TILE, (j + 1) * OUT_TILE)
            gate = gate_ref[cols].reshape(1, OUT_TILE)
            total = product(6, far, at, cols)
            out[at, cols] = (res[at, cols].astype(jnp.float32) + gate * total).astype(out.dtype)

    forward(7, 1, 0)
    shared(2, diagonal, 6).wait_recv()
    for part in range(1, PARTS):
        forward(7, 1, part)
        finish(part - 1)
    shared(1, me, 6).wait_send()
    shared(2, across, 6).wait_send()
    for part in range(PARTS):
        shared(1, me, 7, 1, part).wait_send()
    finish(PARTS - 1)
    for part in range(PARTS):
        shared(2, across, 7, 1, part).wait_send()


def shards(residual, queries, key_rows, value_rows, w_out, out_gate, extents):
    n_t, n_s = lax.axis_size("tensor"), lax.axis_size("seq")
    rows, inner = queries.shape
    tokens, out_cols = residual.shape
    inner_dev = inner // n_t
    heads = inner_dev // HEAD_DIM
    if n_t != 4 or n_s < 2 or rows % 16 or heads != HEADS_DEV or out_cols % OUT_TILE or rows % (4 * PARTS):
        return plain_shards(
            residual, queries, key_rows, value_rows, w_out, out_gate, extents
        )
    frames = tokens // (HT_DEV * WT * TILE)
    half = tokens // HT_DEV
    q_feat, k_feat = mask_features(frames)
    dma = pltpu.SemaphoreType.DMA
    bf16 = jnp.bfloat16
    operands = (
        queries, key_rows, value_rows, w_out.reshape(n_t, heads, HEAD_DIM, out_cols), residual,
        q_feat, k_feat, out_gate, extents.T,
    )
    return pl.pallas_call(
        functools.partial(kernel, n_t, n_s, frames),
        out_shape=pltpu.VMEM((tokens, out_cols), bf16),
        in_specs=[pl.BlockSpec(memory_space=pl.ANY)] * len(operands),
        out_specs=pl.BlockSpec(memory_space=pltpu.VMEM),
        scratch_shapes=[
            pltpu.VMEM((3, tokens, inner_dev), bf16),
            pltpu.VMEM((2, 2, frames, half // frames, inner_dev), bf16),
            pltpu.VMEM((heads, n_t, tokens, HEAD_DIM), bf16),
            pltpu.VMEM((n_t, heads, HEAD_DIM, out_cols), bf16),
            pltpu.VMEM((tokens, out_cols), bf16),
            pltpu.VMEM((tokens, out_cols), jnp.float32),
            pltpu.VMEM(q_feat.shape, bf16),
            pltpu.VMEM(k_feat.shape, bf16),
            pltpu.VMEM(out_gate.shape, jnp.float32),
            pltpu.SMEM(extents.T.shape, jnp.int32),
            dma((len(KV_GROUPS) + len(Q_GROUPS),)),
            dma((len(KV_GROUPS) + len(Q_GROUPS),)),
            dma((3,)),
            dma((2, len(EDGE_GROUPS))),
            dma((2, len(EDGE_GROUPS))),
            dma((3, heads - 1 + PARTS)),
            dma((3, heads - 1 + PARTS)),
            dma((n_t,)),
            dma((5,)),
        ],
        compiler_params=pltpu.CompilerParams(
            collective_id=0, has_side_effects=True, vmem_limit_bytes=40 << 20
        ),
    )(*[pltpu.with_memory_space_constraint(x, pltpu.HBM) for x in operands])


def solution(mesh):
    placed = (
        P("seq", "tensor"),
        P(("seq", "tensor"), None),
        P(("seq", "tensor"), None),
        P(("seq", "tensor"), None),
        P(None, "tensor"),
        P("tensor"),
        P(),
    )
    return jax.shard_map(
        shards, mesh=mesh, in_specs=placed, out_specs=P("seq", "tensor"), check_vma=False
    )
```

```python
import functools
import math

import jax
import jax.numpy as jnp
import numpy as np
from jax import lax
from jax.experimental import pallas as pl
from jax.experimental.pallas import tpu as pltpu
from jax.sharding import PartitionSpec as P

HEAD_DIM = 128
TILE = 32
HT_DEV = 2
WT = 3
HEADS_DEV = 8
CUTS = (0, 288, 576)
PARTS = 2
KV_GROUPS = ((0, 1), (1, 1), (2, 2), (4, 4))
Q_GROUPS = ((0, 2), (2, 6))
EDGE_GROUPS = tuple((h, 1) for h in range(HEADS_DEV))
OUT_TILE = 768
FAR = -1e30
MESH = pl.DeviceIdType.MESH


def passed_along(value, axis, by):
    length = lax.axis_size(axis)
    pairs = [(i, i + by) for i in range(length) if 0 <= i + by < length]
    return lax.ppermute(value, axis, pairs)


def tile_coords(row_count, tile_rows, first_row):
    position = jnp.arange(row_count, dtype=jnp.int32)
    frame_id = position // (tile_rows * WT * TILE)
    row_id = first_row + position // (WT * TILE) % tile_rows
    col_id = position // TILE % WT
    return (frame_id, row_id, col_id)


def allowed_keys(query_place, key_place, head_reach, seq_block, seq_count):
    frame_gap = jnp.abs(query_place[0][:, None] - key_place[0][None, :])
    row_gap = jnp.abs(query_place[1][:, None] - key_place[1][None, :])
    col_gap = jnp.abs(query_place[2][:, None] - key_place[2][None, :])
    global_row = key_place[1] + seq_block * HT_DEV
    inside = (global_row >= 0) & (global_row < seq_count * HT_DEV)
    return (
        (frame_gap[None] <= head_reach[:, 0, None, None])
        & (row_gap[None] <= head_reach[:, 1, None, None])
        & (col_gap[None] <= head_reach[:, 2, None, None])
        & inside[None, None, :]
    )


def plain_shards(residual, queries, key_rows, value_rows, w_out, out_gate, extents):
    head_q, head_k, head_v = (
        lax.all_to_all(queries, "tensor", split_axis=1, concat_axis=0, tiled=True),
        lax.all_to_all(key_rows, "tensor", split_axis=1, concat_axis=0, tiled=True),
        lax.all_to_all(value_rows, "tensor", split_axis=1, concat_axis=0, tiled=True),
    )
    tokens, inner_dev = head_q.shape
    heads_here = inner_dev // HEAD_DIM
    seq_block = lax.axis_index("seq")
    seq_count = lax.axis_size("seq")
    head_reach = lax.dynamic_slice_in_dim(
        extents, lax.axis_index("tensor") * heads_here, heads_here, 0
    )
    query_tiles = head_q.reshape(tokens, heads_here, HEAD_DIM)
    query_place = tile_coords(tokens, HT_DEV, 0)
    stacked = jnp.stack([head_k, head_v])

    def part_scores(pair_rows, key_place):
        key_tiles = pair_rows[0].reshape(-1, heads_here, HEAD_DIM)
        scores = jnp.einsum(
            "qhd,khd->hqk", query_tiles, key_tiles, preferred_element_type=jnp.float32
        ) / math.sqrt(HEAD_DIM)
        allowed = allowed_keys(query_place, key_place, head_reach, seq_block, seq_count)
        return jnp.where(allowed, scores, FAR)

    by_row = stacked.reshape(2, -1, HT_DEV, WT * TILE, inner_dev)
    halves = tokens // HT_DEV
    last_row = by_row[:, :, HT_DEV - 1].reshape(2, halves, inner_dev)
    first_row = by_row[:, :, 0].reshape(2, halves, inner_dev)
    parts = [
        (stacked, query_place),
        (passed_along(last_row, "seq", 1), tile_coords(halves, 1, -1)),
        (passed_along(first_row, "seq", -1), tile_coords(halves, 1, HT_DEV)),
    ]
    scores = jnp.concatenate([part_scores(*part) for part in parts], axis=-1)
    value_all = jnp.concatenate([pair_rows[1] for pair_rows, _ in parts], axis=0)
    row_max = jnp.max(scores, axis=-1, keepdims=True)
    exp_scores = jnp.exp(scores - row_max)
    row_sum = jnp.sum(exp_scores, axis=-1, keepdims=True)
    weights = (exp_scores / row_sum).astype(jnp.bfloat16)
    attended = jnp.einsum(
        "hqk,khd->qhd",
        weights,
        value_all.reshape(-1, heads_here, HEAD_DIM),
        preferred_element_type=jnp.float32,
    )
    head_out = attended.reshape(tokens, inner_dev).astype(jnp.bfloat16)
    projected = jnp.dot(
        lax.all_gather(head_out, "tensor", axis=1, tiled=True),
        w_out,
        preferred_element_type=jnp.float32,
    )
    return (residual.astype(jnp.float32) + out_gate * projected).astype(jnp.bfloat16)


def mask_features(frames):
    span = WT * TILE
    q_feat = np.zeros((2, frames * span, HEAD_DIM), np.float32)
    k_feat = np.zeros((2, frames * 3 * span, HEAD_DIM), np.float32)
    q_at = np.arange(frames * span)
    q_frame, q_col = q_at // span, q_at // TILE % WT
    k_at = np.arange(frames * 3 * span)
    k_frame, k_col = k_at // (3 * span), k_at // TILE % WT
    k_row = k_at // span % 3 - 1
    for r in range(2):
        for j in range(3):
            q_feat[r, :, j] = q_feat[r, :, 8 + j] = q_frame == j
            q_feat[r, :, 3 + j] = q_feat[r, :, 11 + j] = q_col == j
            k_feat[r, :, j] = FAR * (abs(k_frame - j) >= 2)
            k_feat[r, :, 8 + j] = FAR * (abs(k_frame - j) == 1)
            k_feat[r, :, 3 + j] = FAR * (abs(k_col - j) >= 2)
            k_feat[r, :, 11 + j] = FAR * (abs(k_col - j) == 1)
        q_feat[r, :, 14:17] = 1.0
        k_feat[r, :, 14] = FAR * (k_row != 0)
    k_feat[0, :, 15] = FAR * (k_row == -1)
    k_feat[1, :, 16] = FAR * (k_row == 1)
    return jnp.asarray(q_feat, jnp.bfloat16), jnp.asarray(k_feat, jnp.bfloat16)


def kernel(
    n_t, n_s, frames, q_hbm, k_hbm, v_hbm, w_hbm, res_hbm, qf_hbm, kf_hbm, gate_hbm, ext_hbm,
    out, own, halo, gat, wbuf, res, acc, qf, kf, gate_ref, ext_ref,
    a_send, a_recv, a_loc, h_send, h_recv, g_send, g_recv, w_sem, c_sem,
):
    rows = q_hbm.shape[0]
    inner_dev = q_hbm.shape[1] // n_t
    heads = inner_dev // HEAD_DIM
    last = heads - 1
    span = WT * TILE
    me, sb = lax.axis_index("tensor"), lax.axis_index("seq")
    mate = me // 2 * 2 + 1 - lax.rem(me, 2)
    across = lax.rem(me + n_t // 2, n_t)
    near, far = me // 2 * 2, n_t // 2 - me // 2 * 2
    srcs = (k_hbm, v_hbm, q_hbm)
    has_up, has_down = sb < n_s - 1, sb > 0

    barrier = pltpu.get_barrier_semaphore()
    for d in range(1, n_t):
        pl.semaphore_signal(
            barrier, inc=1, device_id={"tensor": lax.rem(me + d, n_t)}, device_id_type=MESH
        )

    @pl.when(has_up)
    def _():
        pl.semaphore_signal(barrier, inc=1, device_id={"seq": sb + 1}, device_id_type=MESH)

    @pl.when(has_down)
    def _():
        pl.semaphore_signal(barrier, inc=1, device_id={"seq": sb - 1}, device_id_type=MESH)

    inner_block = has_up & has_down

    @pl.when(inner_block)
    def _():
        pl.semaphore_wait(barrier, n_t + 1)

    @pl.when(jnp.logical_not(inner_block))
    def _():
        pl.semaphore_wait(barrier, n_t)

    def columns(first, count):
        return pl.ds(pl.multiple_of(first * HEAD_DIM, HEAD_DIM), count * HEAD_DIM)

    def slot(owner):
        return pl.ds(pl.multiple_of(owner * rows, 16), rows)

    def sent(a, d, group, sem):
        first, count = group
        peer = lax.rem(me + d, n_t)
        return pltpu.make_async_remote_copy(
            src_ref=srcs[a].at[:, columns(peer * heads + first, count)],
            dst_ref=own.at[a, slot(me), columns(first, count)],
            send_sem=a_send.at[sem],
            recv_sem=a_recv.at[sem],
            device_id={"tensor": peer},
            device_id_type=MESH,
        )

    def sent_all(arrays, group, sem):
        first, count = group
        ref = own.at[arrays, pl.ds(0, (n_t - 1) * rows), columns(first, count)]
        return pltpu.make_async_remote_copy(
            src_ref=ref,
            dst_ref=ref,
            send_sem=a_send.at[sem],
            recv_sem=a_recv.at[sem],
            device_id={"tensor": mate},
            device_id_type=MESH,
        )

    kv_all = [sent_all(pl.ds(0, 2), g, i) for i, g in enumerate(KV_GROUPS)]
    q_all = [sent_all(pl.ds(2, 1), g, len(KV_GROUPS) + i) for i, g in enumerate(Q_GROUPS)]

    def send_kv(i):
        for a in range(2):
            for d in (2, 3, 1):
                sent(a, d, KV_GROUPS[i], i).start()

    def send_q(i):
        for d in (2, 3, 1):
            sent(2, d, Q_GROUPS[i], len(KV_GROUPS) + i).start()

    kept = [
        pltpu.make_async_copy(
            srcs[a].at[:, columns(me * heads, heads)], own.at[a, slot(me), :], a_loc.at[a]
        )
        for a in range(3)
    ]

    def edges(way, i):
        first, count = EDGE_GROUPS[i]
        by_frame = own.reshape(3, frames, 2 * span, inner_dev)
        return pltpu.make_async_remote_copy(
            src_ref=by_frame.at[
                pl.ds(0, 2), :, pl.ds(span if way == 0 else 0, span), columns(first, count)
            ],
            dst_ref=halo.at[way, :, :, :, columns(first, count)],
            send_sem=h_send.at[way, i],
            recv_sem=h_recv.at[way, i],
            device_id={"seq": sb + 1 if way == 0 else sb - 1},
            device_id_type=MESH,
        )

    def edges_start(i):
        @pl.when(has_up)
        def _():
            edges(0, i).start()

        @pl.when(has_down)
        def _():
            edges(1, i).start()

    def edges_in(i):
        @pl.when(has_down)
        def _():
            edges(0, i).wait_recv()

        @pl.when(has_up)
        def _():
            edges(1, i).wait_recv()

    def edges_out(i):
        @pl.when(has_up)
        def _():
            edges(0, i).wait_send()

        @pl.when(has_down)
        def _():
            edges(1, i).wait_send()

    def shared(kind, piece, first, count=1, part=None):
        if part is None:
            ref, at = gat.at[pl.ds(first, count), piece], first
        else:
            ref = gat.at[first, piece, pl.ds(CUTS[part], CUTS[part + 1] - CUTS[part]), :]
            at = first + part
        return pltpu.make_async_remote_copy(
            src_ref=ref,
            dst_ref=ref,
            send_sem=g_send.at[kind, at],
            recv_sem=g_recv.at[kind, at],
            device_id={"tensor": across if kind == 1 else mate},
            device_id_type=MESH,
        )

    diagonal = lax.rem(mate + n_t // 2, n_t)

    def weights_in(owner):
        return pltpu.make_async_copy(w_hbm.at[owner], wbuf.at[owner], w_sem.at[owner])

    send_kv(0)
    kept[0].start()
    kept[1].start()
    send_kv(1)
    send_kv(2)
    kept[2].start()
    consts = [
        pltpu.make_async_copy(src, dst, c_sem.at[i])
        for i, (src, dst) in enumerate(
            ((qf_hbm, qf), (kf_hbm, kf), (ext_hbm, ext_ref), (gate_hbm, gate_ref), (res_hbm, res))
        )
    ]

    @pl.when(sb == 0)
    def _():
        halo[0] = jnp.zeros(halo.shape[1:], halo.dtype)

    @pl.when(sb == n_s - 1)
    def _():
        halo[1] = jnp.zeros(halo.shape[1:], halo.dtype)

    kept[0].wait()
    kept[1].wait()
    kv_all[0].wait_recv()
    edges_start(0)
    send_q(0)
    send_kv(3)
    send_q(1)
    for copy in consts:
        copy.start()
    for owner in range(n_t):
        weights_in(owner).start()
    kv_all[1].wait_recv()
    edges_start(1)
    acc[...] = jnp.zeros_like(acc)
    kv_all[2].wait_recv()
    edges_start(2)
    edges_start(3)
    for copy in consts:
        copy.wait()
    kept[2].wait()
    for owner in range(n_t):
        weights_in(owner).wait()

    def gathered(a, h, r):
        parts = []
        for f in range(frames):
            here = own[a, f * 2 * span : (f + 1) * 2 * span, columns(h, 1)]
            there = halo[r, a, f, :, columns(h, 1)]
            parts += [there, here] if r == 0 else [here, there]
        return jnp.concatenate(parts, axis=0)

    def switches(head):
        lane = lax.broadcasted_iota(jnp.int32, (1, HEAD_DIM), 1)
        at = me * heads + head
        coef = jnp.where(lane < 8, 1.0, 0.0)
        for d, first, end in ((0, 8, 11), (2, 11, 14), (1, 14, 15)):
            stop = (1 - ext_ref[d, at]).astype(jnp.float32)
            coef = jnp.where((lane >= first) & (lane < end), stop, coef)
        coef = jnp.where(lane == 15, jnp.where(sb == 0, 1.0, 0.0), coef)
        return jnp.where(lane == 16, jnp.where(sb == n_s - 1, 1.0, 0.0), coef)

    def attend(h):
        ones = jnp.ones((frames * 3 * span, HEAD_DIM), jnp.bfloat16)
        coef = switches(h)
        for r in range(2):
            q_part = jnp.concatenate(
                [
                    own[2, (2 * f + r) * span : (2 * f + r + 1) * span, columns(h, 1)]
                    for f in range(frames)
                ],
                axis=0,
            )
            q_feat = (qf[r].astype(jnp.float32) * coef).astype(jnp.bfloat16)
            scores = lax.dot_general(
                jnp.concatenate([q_part, q_feat], axis=1),
                jnp.concatenate([gathered(0, h, r), kf[r]], axis=1),
                (((1,), (1,)), ((), ())),
                preferred_element_type=jnp.float32,
            )
            top = jnp.max(scores, axis=-1, keepdims=True)
            weights = jnp.exp2(
                (scores - top) * (math.log2(math.e) / math.sqrt(HEAD_DIM))
            ).astype(jnp.bfloat16)
            both = jnp.dot(
                weights,
                jnp.concatenate([gathered(1, h, r), ones], axis=1),
                preferred_element_type=jnp.float32,
            )
            done = (both[:, :HEAD_DIM] / both[:, HEAD_DIM:]).astype(jnp.bfloat16)
            for f in range(frames):
                gat[h, me, (2 * f + r) * span : (2 * f + r + 1) * span] = done[
                    f * span : (f + 1) * span
                ]

    def forward(first, count=1, part=None):
        if part is None:
            for h in range(first, first + count):
                shared(1, across, h).wait_recv()
        else:
            shared(1, across, first, count, part).wait_recv()
        shared(2, across, first, count, part).start()

    def product(h, base, at, cols, count=2):
        pieces = [(h + i, base + j) for i in range(count) for j in range(2)]
        lhs = jnp.concatenate([gat[i, j, at] for i, j in pieces], axis=1)
        rhs = jnp.concatenate([wbuf[j, i, :, cols] for i, j in pieces], axis=0)
        return acc[at, cols] + jnp.dot(lhs, rhs, preferred_element_type=jnp.float32)

    def accumulate(h, base):
        @pl.loop(0, acc.shape[1] // OUT_TILE)
        def _(j):
            cols = pl.ds(pl.multiple_of(j * OUT_TILE, OUT_TILE), OUT_TILE)
            acc[:, cols] = product(h, base, slice(None), cols)

    def local(h):
        shared(0, mate, h, 2).wait_recv()
        accumulate(h, near)

    def remote(h):
        shared(2, diagonal, h, 2).wait_recv()
        accumulate(h, far)

    def before(s):
        if s == 2:
            local(0)
            kv_all[3].wait_recv()
            edges_start(4)
            edges_start(5)
            edges_start(6)
            edges_start(7)
        if s == 4:
            local(2)
            for i in range(3):
                kv_all[i].wait_send()
        if s == 5:
            for i in range(3):
                edges_out(i)
            shared(0, me, 0, 2).wait_send()
            shared(0, me, 2, 2).wait_send()
        if s == 6:
            local(4)
            for i in range(2):
                q_all[i].wait_send()
            kv_all[3].wait_send()
            forward(0, 2)
        if s == 7:
            for i in range(3, 6):
                edges_out(i)
            shared(0, me, 4, 2).wait_send()
            shared(1, me, 0).wait_send()
            shared(1, me, 1).wait_send()
            remote(0)
            forward(2, 2)
            shared(2, across, 0, 2).wait_send()
        if s in (0, 2, 4):
            if s < 4:
                q_all[s // 2].wait_recv()
        for i, (first, _) in enumerate(EDGE_GROUPS):
            if first == s:
                edges_in(i)

    def after(s):
        if s < 7:
            shared(1, me, s).start()
        if s == 7:
            for part in range(PARTS):
                shared(1, me, 7, 1, part).start()
        if s % 2:
            shared(0, me, s - 1, 2).start()

    @pl.loop(0, heads)
    def _(s):
        for i in range(HEADS_DEV):
            pl.when(s == i)(functools.partial(before, i))

        attend(s)

        for i in range(HEADS_DEV):
            pl.when(s == i)(functools.partial(after, i))

    remote(2)
    forward(4, 2)
    local(6)
    shared(1, me, 2).wait_send()
    shared(1, me, 3).wait_send()
    shared(2, across, 2, 2).wait_send()
    remote(4)
    edges_out(6)
    edges_out(7)
    forward(6)
    shared(0, me, 6, 2).wait_send()
    shared(1, me, 4).wait_send()
    shared(1, me, 5).wait_send()
    shared(2, across, 4, 2).wait_send()

    def finish(part, first):
        shared(2, diagonal, 7, 1, part).wait_recv()
        at = slice(CUTS[part], CUTS[part + 1])
        for j in range(acc.shape[1] // OUT_TILE):
            cols = slice(j * OUT_TILE, (j + 1) * OUT_TILE)
            gate = gate_ref[cols].reshape(1, OUT_TILE)
            total = product(first, far, at, cols, 8 - first)
            out[at, cols] = (res[at, cols].astype(jnp.float32) + gate * total).astype(out.dtype)

    forward(7, 1, 0)
    shared(2, diagonal, 6).wait_recv()
    for part in range(1, PARTS):
        forward(7, 1, part)
        finish(part - 1, 6 if part == 1 else 7)
        if part == 1:
            at = slice(CUTS[1], CUTS[PARTS])
            for j in range(acc.shape[1] // OUT_TILE):
                cols = slice(j * OUT_TILE, (j + 1) * OUT_TILE)
                acc[at, cols] = product(6, far, at, cols, 1)
    shared(1, me, 6).wait_send()
    shared(2, across, 6).wait_send()
    for part in range(PARTS):
        shared(1, me, 7, 1, part).wait_send()
    finish(PARTS - 1, 7)
    for part in range(PARTS):
        shared(2, across, 7, 1, part).wait_send()


def shards(residual, queries, key_rows, value_rows, w_out, out_gate, extents):
    n_t, n_s = lax.axis_size("tensor"), lax.axis_size("seq")
    rows, inner = queries.shape
    tokens, out_cols = residual.shape
    inner_dev = inner // n_t
    heads = inner_dev // HEAD_DIM
    if n_t != 4 or n_s < 2 or rows % 16 or heads != HEADS_DEV or out_cols % OUT_TILE or rows % (4 * PARTS):
        return plain_shards(
            residual, queries, key_rows, value_rows, w_out, out_gate, extents
        )
    frames = tokens // (HT_DEV * WT * TILE)
    half = tokens // HT_DEV
    q_feat, k_feat = mask_features(frames)
    dma = pltpu.SemaphoreType.DMA
    bf16 = jnp.bfloat16
    operands = (
        queries, key_rows, value_rows, w_out.reshape(n_t, heads, HEAD_DIM, out_cols), residual,
        q_feat, k_feat, out_gate, extents.T,
    )
    return pl.pallas_call(
        functools.partial(kernel, n_t, n_s, frames),
        out_shape=pltpu.VMEM((tokens, out_cols), bf16),
        in_specs=[pl.BlockSpec(memory_space=pl.ANY)] * len(operands),
        out_specs=pl.BlockSpec(memory_space=pltpu.VMEM),
        scratch_shapes=[
            pltpu.VMEM((3, tokens, inner_dev), bf16),
            pltpu.VMEM((2, 2, frames, half // frames, inner_dev), bf16),
            pltpu.VMEM((heads, n_t, tokens, HEAD_DIM), bf16),
            pltpu.VMEM((n_t, heads, HEAD_DIM, out_cols), bf16),
            pltpu.VMEM((tokens, out_cols), bf16),
            pltpu.VMEM((tokens, out_cols), jnp.float32),
            pltpu.VMEM(q_feat.shape, bf16),
            pltpu.VMEM(k_feat.shape, bf16),
            pltpu.VMEM(out_gate.shape, jnp.float32),
            pltpu.SMEM(extents.T.shape, jnp.int32),
            dma((len(KV_GROUPS) + len(Q_GROUPS),)),
            dma((len(KV_GROUPS) + len(Q_GROUPS),)),
            dma((3,)),
            dma((2, len(EDGE_GROUPS))),
            dma((2, len(EDGE_GROUPS))),
            dma((3, heads - 1 + PARTS)),
            dma((3, heads - 1 + PARTS)),
            dma((n_t,)),
            dma((5,)),
        ],
        compiler_params=pltpu.CompilerParams(
            collective_id=0, has_side_effects=True, vmem_limit_bytes=40 << 20
        ),
    )(*[pltpu.with_memory_space_constraint(x, pltpu.HBM) for x in operands])


def solution(mesh):
    placed = (
        P("seq", "tensor"),
        P(("seq", "tensor"), None),
        P(("seq", "tensor"), None),
        P(("seq", "tensor"), None),
        P(None, "tensor"),
        P("tensor"),
        P(),
    )
    return jax.shard_map(
        shards, mesh=mesh, in_specs=placed, out_specs=P("seq", "tensor"), check_vma=False
    )
```

```python
import functools
import math

import jax
import jax.numpy as jnp
import numpy as np
from jax import lax
from jax.experimental import pallas as pl
from jax.experimental.pallas import tpu as pltpu
from jax.sharding import PartitionSpec as P

HEAD_DIM = 128
TILE = 32
HT_DEV = 2
WT = 3
HEADS_DEV = 8
CUTS = (0, 288, 576)
PARTS = 2
KV_GROUPS = ((0, 1), (1, 1), (2, 2), (4, 4))
Q_GROUPS = ((0, 2), (2, 6))
EDGE_GROUPS = tuple((h, 1) for h in range(HEADS_DEV))
OUT_TILE = 768
FAR = -1e30
MESH = pl.DeviceIdType.MESH


def passed_along(value, axis, by):
    length = lax.axis_size(axis)
    pairs = [(i, i + by) for i in range(length) if 0 <= i + by < length]
    return lax.ppermute(value, axis, pairs)


def tile_coords(row_count, tile_rows, first_row):
    position = jnp.arange(row_count, dtype=jnp.int32)
    frame_id = position // (tile_rows * WT * TILE)
    row_id = first_row + position // (WT * TILE) % tile_rows
    col_id = position // TILE % WT
    return (frame_id, row_id, col_id)


def allowed_keys(query_place, key_place, head_reach, seq_block, seq_count):
    frame_gap = jnp.abs(query_place[0][:, None] - key_place[0][None, :])
    row_gap = jnp.abs(query_place[1][:, None] - key_place[1][None, :])
    col_gap = jnp.abs(query_place[2][:, None] - key_place[2][None, :])
    global_row = key_place[1] + seq_block * HT_DEV
    inside = (global_row >= 0) & (global_row < seq_count * HT_DEV)
    return (
        (frame_gap[None] <= head_reach[:, 0, None, None])
        & (row_gap[None] <= head_reach[:, 1, None, None])
        & (col_gap[None] <= head_reach[:, 2, None, None])
        & inside[None, None, :]
    )


def plain_shards(residual, queries, key_rows, value_rows, w_out, out_gate, extents):
    head_q, head_k, head_v = (
        lax.all_to_all(queries, "tensor", split_axis=1, concat_axis=0, tiled=True),
        lax.all_to_all(key_rows, "tensor", split_axis=1, concat_axis=0, tiled=True),
        lax.all_to_all(value_rows, "tensor", split_axis=1, concat_axis=0, tiled=True),
    )
    tokens, inner_dev = head_q.shape
    heads_here = inner_dev // HEAD_DIM
    seq_block = lax.axis_index("seq")
    seq_count = lax.axis_size("seq")
    head_reach = lax.dynamic_slice_in_dim(
        extents, lax.axis_index("tensor") * heads_here, heads_here, 0
    )
    query_tiles = head_q.reshape(tokens, heads_here, HEAD_DIM)
    query_place = tile_coords(tokens, HT_DEV, 0)
    stacked = jnp.stack([head_k, head_v])

    def part_scores(pair_rows, key_place):
        key_tiles = pair_rows[0].reshape(-1, heads_here, HEAD_DIM)
        scores = jnp.einsum(
            "qhd,khd->hqk", query_tiles, key_tiles, preferred_element_type=jnp.float32
        ) / math.sqrt(HEAD_DIM)
        allowed = allowed_keys(query_place, key_place, head_reach, seq_block, seq_count)
        return jnp.where(allowed, scores, FAR)

    by_row = stacked.reshape(2, -1, HT_DEV, WT * TILE, inner_dev)
    halves = tokens // HT_DEV
    last_row = by_row[:, :, HT_DEV - 1].reshape(2, halves, inner_dev)
    first_row = by_row[:, :, 0].reshape(2, halves, inner_dev)
    parts = [
        (stacked, query_place),
        (passed_along(last_row, "seq", 1), tile_coords(halves, 1, -1)),
        (passed_along(first_row, "seq", -1), tile_coords(halves, 1, HT_DEV)),
    ]
    scores = jnp.concatenate([part_scores(*part) for part in parts], axis=-1)
    value_all = jnp.concatenate([pair_rows[1] for pair_rows, _ in parts], axis=0)
    row_max = jnp.max(scores, axis=-1, keepdims=True)
    exp_scores = jnp.exp(scores - row_max)
    row_sum = jnp.sum(exp_scores, axis=-1, keepdims=True)
    weights = (exp_scores / row_sum).astype(jnp.bfloat16)
    attended = jnp.einsum(
        "hqk,khd->qhd",
        weights,
        value_all.reshape(-1, heads_here, HEAD_DIM),
        preferred_element_type=jnp.float32,
    )
    head_out = attended.reshape(tokens, inner_dev).astype(jnp.bfloat16)
    projected = jnp.dot(
        lax.all_gather(head_out, "tensor", axis=1, tiled=True),
        w_out,
        preferred_element_type=jnp.float32,
    )
    return (residual.astype(jnp.float32) + out_gate * projected).astype(jnp.bfloat16)


def mask_features(frames):
    span = WT * TILE
    q_feat = np.zeros((2, frames * span, HEAD_DIM), np.float32)
    k_feat = np.zeros((2, frames * 3 * span, HEAD_DIM), np.float32)
    q_at = np.arange(frames * span)
    q_frame, q_col = q_at // span, q_at // TILE % WT
    k_at = np.arange(frames * 3 * span)
    k_frame, k_col = k_at // (3 * span), k_at // TILE % WT
    k_row = k_at // span % 3 - 1
    for r in range(2):
        for j in range(3):
            q_feat[r, :, j] = q_feat[r, :, 8 + j] = q_frame == j
            q_feat[r, :, 3 + j] = q_feat[r, :, 11 + j] = q_col == j
            k_feat[r, :, j] = FAR * (abs(k_frame - j) >= 2)
            k_feat[r, :, 8 + j] = FAR * (abs(k_frame - j) == 1)
            k_feat[r, :, 3 + j] = FAR * (abs(k_col - j) >= 2)
            k_feat[r, :, 11 + j] = FAR * (abs(k_col - j) == 1)
        q_feat[r, :, 14:17] = 1.0
        k_feat[r, :, 14] = FAR * (k_row != 0)
    k_feat[0, :, 15] = FAR * (k_row == -1)
    k_feat[1, :, 16] = FAR * (k_row == 1)
    return jnp.asarray(q_feat, jnp.bfloat16), jnp.asarray(k_feat, jnp.bfloat16)


def kernel(
    n_t, n_s, frames, q_hbm, k_hbm, v_hbm, w_hbm, res_hbm, qf_hbm, kf_hbm, gate_hbm, ext_hbm,
    out, own, halo, gat, wbuf, res, acc, qf, kf, gate_ref, ext_ref,
    a_send, a_recv, a_loc, h_send, h_recv, g_send, g_recv, w_sem, c_sem,
):
    rows = q_hbm.shape[0]
    inner_dev = q_hbm.shape[1] // n_t
    heads = inner_dev // HEAD_DIM
    last = heads - 1
    span = WT * TILE
    me, sb = lax.axis_index("tensor"), lax.axis_index("seq")
    mate = me // 2 * 2 + 1 - lax.rem(me, 2)
    across = lax.rem(me + n_t // 2, n_t)
    near, far = me // 2 * 2, n_t // 2 - me // 2 * 2
    srcs = (k_hbm, v_hbm, q_hbm)
    has_up, has_down = sb < n_s - 1, sb > 0

    barrier = pltpu.get_barrier_semaphore()
    for d in range(1, n_t):
        pl.semaphore_signal(
            barrier, inc=1, device_id={"tensor": lax.rem(me + d, n_t)}, device_id_type=MESH
        )

    @pl.when(has_up)
    def _():
        pl.semaphore_signal(barrier, inc=1, device_id={"seq": sb + 1}, device_id_type=MESH)

    @pl.when(has_down)
    def _():
        pl.semaphore_signal(barrier, inc=1, device_id={"seq": sb - 1}, device_id_type=MESH)

    inner_block = has_up & has_down

    @pl.when(inner_block)
    def _():
        pl.semaphore_wait(barrier, n_t + 1)

    @pl.when(jnp.logical_not(inner_block))
    def _():
        pl.semaphore_wait(barrier, n_t)

    def columns(first, count):
        return pl.ds(pl.multiple_of(first * HEAD_DIM, HEAD_DIM), count * HEAD_DIM)

    def slot(owner):
        return pl.ds(pl.multiple_of(owner * rows, 16), rows)

    def sent(a, d, group, sem):
        first, count = group
        peer = lax.rem(me + d, n_t)
        return pltpu.make_async_remote_copy(
            src_ref=srcs[a].at[:, columns(peer * heads + first, count)],
            dst_ref=own.at[a, slot(me), columns(first, count)],
            send_sem=a_send.at[sem],
            recv_sem=a_recv.at[sem],
            device_id={"tensor": peer},
            device_id_type=MESH,
        )

    def sent_all(arrays, group, sem):
        first, count = group
        ref = own.at[arrays, pl.ds(0, (n_t - 1) * rows), columns(first, count)]
        return pltpu.make_async_remote_copy(
            src_ref=ref,
            dst_ref=ref,
            send_sem=a_send.at[sem],
            recv_sem=a_recv.at[sem],
            device_id={"tensor": mate},
            device_id_type=MESH,
        )

    kv_all = [sent_all(pl.ds(0, 2), g, i) for i, g in enumerate(KV_GROUPS)]
    q_all = [sent_all(pl.ds(2, 1), g, len(KV_GROUPS) + i) for i, g in enumerate(Q_GROUPS)]

    def send_kv(i):
        for a in range(2):
            for d in (3, 2, 1):
                sent(a, d, KV_GROUPS[i], i).start()

    def send_q(i):
        for d in (3, 2, 1):
            sent(2, d, Q_GROUPS[i], len(KV_GROUPS) + i).start()

    kept = [
        pltpu.make_async_copy(
            srcs[a].at[:, columns(me * heads, heads)], own.at[a, slot(me), :], a_loc.at[a]
        )
        for a in range(3)
    ]

    def edges(way, i):
        first, count = EDGE_GROUPS[i]
        by_frame = own.reshape(3, frames, 2 * span, inner_dev)
        return pltpu.make_async_remote_copy(
            src_ref=by_frame.at[
                pl.ds(0, 2), :, pl.ds(span if way == 0 else 0, span), columns(first, count)
            ],
            dst_ref=halo.at[way, :, :, :, columns(first, count)],
            send_sem=h_send.at[way, i],
            recv_sem=h_recv.at[way, i],
            device_id={"seq": sb + 1 if way == 0 else sb - 1},
            device_id_type=MESH,
        )

    def edges_start(i):
        @pl.when(has_up)
        def _():
            edges(0, i).start()

        @pl.when(has_down)
        def _():
            edges(1, i).start()

    def edges_in(i):
        @pl.when(has_down)
        def _():
            edges(0, i).wait_recv()

        @pl.when(has_up)
        def _():
            edges(1, i).wait_recv()

    def edges_out(i):
        @pl.when(has_up)
        def _():
            edges(0, i).wait_send()

        @pl.when(has_down)
        def _():
            edges(1, i).wait_send()

    def shared(kind, piece, first, count=1, part=None):
        if part is None:
            ref, at = gat.at[pl.ds(first, count), piece], first
        else:
            ref = gat.at[first, piece, pl.ds(CUTS[part], CUTS[part + 1] - CUTS[part]), :]
            at = first + part
        return pltpu.make_async_remote_copy(
            src_ref=ref,
            dst_ref=ref,
            send_sem=g_send.at[kind, at],
            recv_sem=g_recv.at[kind, at],
            device_id={"tensor": across if kind == 1 else mate},
            device_id_type=MESH,
        )

    diagonal = lax.rem(mate + n_t // 2, n_t)

    def weights_in(owner):
        return pltpu.make_async_copy(w_hbm.at[owner], wbuf.at[owner], w_sem.at[owner])

    send_kv(0)
    kept[0].start()
    kept[1].start()
    send_kv(1)
    send_kv(2)
    kept[2].start()
    consts = [
        pltpu.make_async_copy(src, dst, c_sem.at[i])
        for i, (src, dst) in enumerate(
            ((qf_hbm, qf), (kf_hbm, kf), (ext_hbm, ext_ref), (gate_hbm, gate_ref), (res_hbm, res))
        )
    ]

    @pl.when(sb == 0)
    def _():
        halo[0] = jnp.zeros(halo.shape[1:], halo.dtype)

    @pl.when(sb == n_s - 1)
    def _():
        halo[1] = jnp.zeros(halo.shape[1:], halo.dtype)

    kept[0].wait()
    kept[1].wait()
    kv_all[0].wait_recv()
    edges_start(0)
    send_q(0)
    send_kv(3)
    send_q(1)
    for copy in consts:
        copy.start()
    for owner in range(n_t):
        weights_in(owner).start()
    kv_all[1].wait_recv()
    edges_start(1)
    acc[...] = jnp.zeros_like(acc)
    kv_all[2].wait_recv()
    edges_start(2)
    edges_start(3)
    for copy in consts:
        copy.wait()
    kept[2].wait()
    for owner in range(n_t):
        weights_in(owner).wait()

    def gathered(a, h, r):
        parts = []
        for f in range(frames):
            here = own[a, f * 2 * span : (f + 1) * 2 * span, columns(h, 1)]
            there = halo[r, a, f, :, columns(h, 1)]
            parts += [there, here] if r == 0 else [here, there]
        return jnp.concatenate(parts, axis=0)

    def switches(head):
        lane = lax.broadcasted_iota(jnp.int32, (1, HEAD_DIM), 1)
        at = me * heads + head
        coef = jnp.where(lane < 8, 1.0, 0.0)
        for d, first, end in ((0, 8, 11), (2, 11, 14), (1, 14, 15)):
            stop = (1 - ext_ref[d, at]).astype(jnp.float32)
            coef = jnp.where((lane >= first) & (lane < end), stop, coef)
        coef = jnp.where(lane == 15, jnp.where(sb == 0, 1.0, 0.0), coef)
        return jnp.where(lane == 16, jnp.where(sb == n_s - 1, 1.0, 0.0), coef)

    def attend(h):
        ones = jnp.ones((frames * 3 * span, HEAD_DIM), jnp.bfloat16)
        coef = switches(h)
        for r in range(2):
            q_part = jnp.concatenate(
                [
                    own[2, (2 * f + r) * span : (2 * f + r + 1) * span, columns(h, 1)]
                    for f in range(frames)
                ],
                axis=0,
            )
            q_feat = (qf[r].astype(jnp.float32) * coef).astype(jnp.bfloat16)
            scores = lax.dot_general(
                jnp.concatenate([q_part, q_feat], axis=1),
                jnp.concatenate([gathered(0, h, r), kf[r]], axis=1),
                (((1,), (1,)), ((), ())),
                preferred_element_type=jnp.float32,
            )
            top = jnp.max(scores, axis=-1, keepdims=True)
            weights = jnp.exp2(
                (scores - top) * (math.log2(math.e) / math.sqrt(HEAD_DIM))
            ).astype(jnp.bfloat16)
            both = jnp.dot(
                weights,
                jnp.concatenate([gathered(1, h, r), ones], axis=1),
                preferred_element_type=jnp.float32,
            )
            done = (both[:, :HEAD_DIM] / both[:, HEAD_DIM:]).astype(jnp.bfloat16)
            for f in range(frames):
                gat[h, me, (2 * f + r) * span : (2 * f + r + 1) * span] = done[
                    f * span : (f + 1) * span
                ]

    def forward(first, count=1, part=None):
        if part is None:
            for h in range(first, first + count):
                shared(1, across, h).wait_recv()
        else:
            shared(1, across, first, count, part).wait_recv()
        shared(2, across, first, count, part).start()

    def product(h, base, at, cols, count=2):
        pieces = [(h + i, base + j) for i in range(count) for j in range(2)]
        lhs = jnp.concatenate([gat[i, j, at] for i, j in pieces], axis=1)
        rhs = jnp.concatenate([wbuf[j, i, :, cols] for i, j in pieces], axis=0)
        return acc[at, cols] + jnp.dot(lhs, rhs, preferred_element_type=jnp.float32)

    def accumulate(h, base):
        @pl.loop(0, acc.shape[1] // OUT_TILE)
        def _(j):
            cols = pl.ds(pl.multiple_of(j * OUT_TILE, OUT_TILE), OUT_TILE)
            acc[:, cols] = product(h, base, slice(None), cols)

    def local(h):
        shared(0, mate, h, 2).wait_recv()
        accumulate(h, near)

    def remote(h):
        shared(2, diagonal, h, 2).wait_recv()
        accumulate(h, far)

    def before(s):
        if s == 2:
            local(0)
            kv_all[3].wait_recv()
            edges_start(4)
            edges_start(5)
            edges_start(6)
            edges_start(7)
        if s == 4:
            local(2)
            for i in range(3):
                kv_all[i].wait_send()
        if s == 5:
            for i in range(3):
                edges_out(i)
            shared(0, me, 0, 2).wait_send()
            shared(0, me, 2, 2).wait_send()
        if s == 6:
            local(4)
            for i in range(2):
                q_all[i].wait_send()
            kv_all[3].wait_send()
            forward(0, 2)
        if s == 7:
            for i in range(3, 6):
                edges_out(i)
            shared(0, me, 4, 2).wait_send()
            shared(1, me, 0).wait_send()
            shared(1, me, 1).wait_send()
            remote(0)
            forward(2, 2)
            shared(2, across, 0, 2).wait_send()
        if s in (0, 2, 4):
            if s < 4:
                q_all[s // 2].wait_recv()
        for i, (first, _) in enumerate(EDGE_GROUPS):
            if first == s:
                edges_in(i)

    def after(s):
        if s < 7:
            shared(1, me, s).start()
        if s == 7:
            for part in range(PARTS):
                shared(1, me, 7, 1, part).start()
        if s % 2:
            shared(0, me, s - 1, 2).start()

    @pl.loop(0, heads)
    def _(s):
        for i in range(HEADS_DEV):
            pl.when(s == i)(functools.partial(before, i))

        attend(s)

        for i in range(HEADS_DEV):
            pl.when(s == i)(functools.partial(after, i))

    remote(2)
    forward(4, 2)
    local(6)
    shared(1, me, 2).wait_send()
    shared(1, me, 3).wait_send()
    shared(2, across, 2, 2).wait_send()
    remote(4)
    edges_out(6)
    edges_out(7)
    forward(6)
    shared(0, me, 6, 2).wait_send()
    shared(1, me, 4).wait_send()
    shared(1, me, 5).wait_send()
    shared(2, across, 4, 2).wait_send()

    def finish(part, first):
        shared(2, diagonal, 7, 1, part).wait_recv()
        at = slice(CUTS[part], CUTS[part + 1])
        for j in range(acc.shape[1] // OUT_TILE):
            cols = slice(j * OUT_TILE, (j + 1) * OUT_TILE)
            gate = gate_ref[cols].reshape(1, OUT_TILE)
            total = product(first, far, at, cols, 8 - first)
            out[at, cols] = (res[at, cols].astype(jnp.float32) + gate * total).astype(out.dtype)

    forward(7, 1, 0)
    shared(2, diagonal, 6).wait_recv()
    for part in range(1, PARTS):
        forward(7, 1, part)
        finish(part - 1, 6 if part == 1 else 7)
        if part == 1:
            at = slice(CUTS[1], CUTS[PARTS])
            for j in range(acc.shape[1] // OUT_TILE):
                cols = slice(j * OUT_TILE, (j + 1) * OUT_TILE)
                acc[at, cols] = product(6, far, at, cols, 1)
    shared(1, me, 6).wait_send()
    shared(2, across, 6).wait_send()
    for part in range(PARTS):
        shared(1, me, 7, 1, part).wait_send()
    finish(PARTS - 1, 7)
    for part in range(PARTS):
        shared(2, across, 7, 1, part).wait_send()


def shards(residual, queries, key_rows, value_rows, w_out, out_gate, extents):
    n_t, n_s = lax.axis_size("tensor"), lax.axis_size("seq")
    rows, inner = queries.shape
    tokens, out_cols = residual.shape
    inner_dev = inner // n_t
    heads = inner_dev // HEAD_DIM
    if n_t != 4 or n_s < 2 or rows % 16 or heads != HEADS_DEV or out_cols % OUT_TILE or rows % (4 * PARTS):
        return plain_shards(
            residual, queries, key_rows, value_rows, w_out, out_gate, extents
        )
    frames = tokens // (HT_DEV * WT * TILE)
    half = tokens // HT_DEV
    q_feat, k_feat = mask_features(frames)
    dma = pltpu.SemaphoreType.DMA
    bf16 = jnp.bfloat16
    operands = (
        queries, key_rows, value_rows, w_out.reshape(n_t, heads, HEAD_DIM, out_cols), residual,
        q_feat, k_feat, out_gate, extents.T,
    )
    return pl.pallas_call(
        functools.partial(kernel, n_t, n_s, frames),
        out_shape=pltpu.VMEM((tokens, out_cols), bf16),
        in_specs=[pl.BlockSpec(memory_space=pl.ANY)] * len(operands),
        out_specs=pl.BlockSpec(memory_space=pltpu.VMEM),
        scratch_shapes=[
            pltpu.VMEM((3, tokens, inner_dev), bf16),
            pltpu.VMEM((2, 2, frames, half // frames, inner_dev), bf16),
            pltpu.VMEM((heads, n_t, tokens, HEAD_DIM), bf16),
            pltpu.VMEM((n_t, heads, HEAD_DIM, out_cols), bf16),
            pltpu.VMEM((tokens, out_cols), bf16),
            pltpu.VMEM((tokens, out_cols), jnp.float32),
            pltpu.VMEM(q_feat.shape, bf16),
            pltpu.VMEM(k_feat.shape, bf16),
            pltpu.VMEM(out_gate.shape, jnp.float32),
            pltpu.SMEM(extents.T.shape, jnp.int32),
            dma((len(KV_GROUPS) + len(Q_GROUPS),)),
            dma((len(KV_GROUPS) + len(Q_GROUPS),)),
            dma((3,)),
            dma((2, len(EDGE_GROUPS))),
            dma((2, len(EDGE_GROUPS))),
            dma((3, heads - 1 + PARTS)),
            dma((3, heads - 1 + PARTS)),
            dma((n_t,)),
            dma((5,)),
        ],
        compiler_params=pltpu.CompilerParams(
            collective_id=0, has_side_effects=True, vmem_limit_bytes=40 << 20
        ),
    )(*[pltpu.with_memory_space_constraint(x, pltpu.HBM) for x in operands])


def solution(mesh):
    placed = (
        P("seq", "tensor"),
        P(("seq", "tensor"), None),
        P(("seq", "tensor"), None),
        P(("seq", "tensor"), None),
        P(None, "tensor"),
        P("tensor"),
        P(),
    )
    return jax.shard_map(
        shards, mesh=mesh, in_specs=placed, out_specs=P("seq", "tensor"), check_vma=False
    )
```

```python
import functools
import math

import jax
import jax.numpy as jnp
import numpy as np
from jax import lax
from jax.experimental import pallas as pl
from jax.experimental.pallas import tpu as pltpu
from jax.sharding import PartitionSpec as P

HEAD_DIM = 128
TILE = 32
HT_DEV = 2
WT = 3
HEADS_DEV = 8
CUTS = (0, 288, 576)
PARTS = 2
KV_GROUPS = ((0, 1), (1, 1), (2, 2), (4, 4))
Q_GROUPS = ((0, 2), (2, 6))
EDGE_GROUPS = tuple((h, 1) for h in range(HEADS_DEV))
OUT_TILE = 768
FAR = -1e30
MESH = pl.DeviceIdType.MESH


def passed_along(value, axis, by):
    length = lax.axis_size(axis)
    pairs = [(i, i + by) for i in range(length) if 0 <= i + by < length]
    return lax.ppermute(value, axis, pairs)


def tile_coords(row_count, tile_rows, first_row):
    position = jnp.arange(row_count, dtype=jnp.int32)
    frame_id = position // (tile_rows * WT * TILE)
    row_id = first_row + position // (WT * TILE) % tile_rows
    col_id = position // TILE % WT
    return (frame_id, row_id, col_id)


def allowed_keys(query_place, key_place, head_reach, seq_block, seq_count):
    frame_gap = jnp.abs(query_place[0][:, None] - key_place[0][None, :])
    row_gap = jnp.abs(query_place[1][:, None] - key_place[1][None, :])
    col_gap = jnp.abs(query_place[2][:, None] - key_place[2][None, :])
    global_row = key_place[1] + seq_block * HT_DEV
    inside = (global_row >= 0) & (global_row < seq_count * HT_DEV)
    return (
        (frame_gap[None] <= head_reach[:, 0, None, None])
        & (row_gap[None] <= head_reach[:, 1, None, None])
        & (col_gap[None] <= head_reach[:, 2, None, None])
        & inside[None, None, :]
    )


def plain_shards(residual, queries, key_rows, value_rows, w_out, out_gate, extents):
    head_q, head_k, head_v = (
        lax.all_to_all(queries, "tensor", split_axis=1, concat_axis=0, tiled=True),
        lax.all_to_all(key_rows, "tensor", split_axis=1, concat_axis=0, tiled=True),
        lax.all_to_all(value_rows, "tensor", split_axis=1, concat_axis=0, tiled=True),
    )
    tokens, inner_dev = head_q.shape
    heads_here = inner_dev // HEAD_DIM
    seq_block = lax.axis_index("seq")
    seq_count = lax.axis_size("seq")
    head_reach = lax.dynamic_slice_in_dim(
        extents, lax.axis_index("tensor") * heads_here, heads_here, 0
    )
    query_tiles = head_q.reshape(tokens, heads_here, HEAD_DIM)
    query_place = tile_coords(tokens, HT_DEV, 0)
    stacked = jnp.stack([head_k, head_v])

    def part_scores(pair_rows, key_place):
        key_tiles = pair_rows[0].reshape(-1, heads_here, HEAD_DIM)
        scores = jnp.einsum(
            "qhd,khd->hqk", query_tiles, key_tiles, preferred_element_type=jnp.float32
        ) / math.sqrt(HEAD_DIM)
        allowed = allowed_keys(query_place, key_place, head_reach, seq_block, seq_count)
        return jnp.where(allowed, scores, FAR)

    by_row = stacked.reshape(2, -1, HT_DEV, WT * TILE, inner_dev)
    halves = tokens // HT_DEV
    last_row = by_row[:, :, HT_DEV - 1].reshape(2, halves, inner_dev)
    first_row = by_row[:, :, 0].reshape(2, halves, inner_dev)
    parts = [
        (stacked, query_place),
        (passed_along(last_row, "seq", 1), tile_coords(halves, 1, -1)),
        (passed_along(first_row, "seq", -1), tile_coords(halves, 1, HT_DEV)),
    ]
    scores = jnp.concatenate([part_scores(*part) for part in parts], axis=-1)
    value_all = jnp.concatenate([pair_rows[1] for pair_rows, _ in parts], axis=0)
    row_max = jnp.max(scores, axis=-1, keepdims=True)
    exp_scores = jnp.exp(scores - row_max)
    row_sum = jnp.sum(exp_scores, axis=-1, keepdims=True)
    weights = (exp_scores / row_sum).astype(jnp.bfloat16)
    attended = jnp.einsum(
        "hqk,khd->qhd",
        weights,
        value_all.reshape(-1, heads_here, HEAD_DIM),
        preferred_element_type=jnp.float32,
    )
    head_out = attended.reshape(tokens, inner_dev).astype(jnp.bfloat16)
    projected = jnp.dot(
        lax.all_gather(head_out, "tensor", axis=1, tiled=True),
        w_out,
        preferred_element_type=jnp.float32,
    )
    return (residual.astype(jnp.float32) + out_gate * projected).astype(jnp.bfloat16)


def mask_features(frames):
    span = WT * TILE
    q_feat = np.zeros((2, frames * span, HEAD_DIM), np.float32)
    k_feat = np.zeros((2, frames * 3 * span, HEAD_DIM), np.float32)
    q_at = np.arange(frames * span)
    q_frame, q_col = q_at // span, q_at // TILE % WT
    k_at = np.arange(frames * 3 * span)
    k_frame, k_col = k_at // (3 * span), k_at // TILE % WT
    k_row = k_at // span % 3 - 1
    for r in range(2):
        for j in range(3):
            q_feat[r, :, j] = q_feat[r, :, 8 + j] = q_frame == j
            q_feat[r, :, 3 + j] = q_feat[r, :, 11 + j] = q_col == j
            k_feat[r, :, j] = FAR * (abs(k_frame - j) >= 2)
            k_feat[r, :, 8 + j] = FAR * (abs(k_frame - j) == 1)
            k_feat[r, :, 3 + j] = FAR * (abs(k_col - j) >= 2)
            k_feat[r, :, 11 + j] = FAR * (abs(k_col - j) == 1)
        q_feat[r, :, 14:17] = 1.0
        k_feat[r, :, 14] = FAR * (k_row != 0)
    k_feat[0, :, 15] = FAR * (k_row == -1)
    k_feat[1, :, 16] = FAR * (k_row == 1)
    return jnp.asarray(q_feat, jnp.bfloat16), jnp.asarray(k_feat, jnp.bfloat16)


def kernel(
    n_t, n_s, frames, q_hbm, k_hbm, v_hbm, w_hbm, res_hbm, qf_hbm, kf_hbm, gate_hbm, ext_hbm,
    out, own, halo, gat, wbuf, res, acc, qf, kf, gate_ref, ext_ref,
    a_send, a_recv, a_loc, h_send, h_recv, g_send, g_recv, w_sem, c_sem,
):
    rows = q_hbm.shape[0]
    inner_dev = q_hbm.shape[1] // n_t
    heads = inner_dev // HEAD_DIM
    last = heads - 1
    span = WT * TILE
    me, sb = lax.axis_index("tensor"), lax.axis_index("seq")
    mate = me // 2 * 2 + 1 - lax.rem(me, 2)
    across = lax.rem(me + n_t // 2, n_t)
    near, far = me // 2 * 2, n_t // 2 - me // 2 * 2
    srcs = (k_hbm, v_hbm, q_hbm)
    has_up, has_down = sb < n_s - 1, sb > 0

    barrier = pltpu.get_barrier_semaphore()
    for d in range(1, n_t):
        pl.semaphore_signal(
            barrier, inc=1, device_id={"tensor": lax.rem(me + d, n_t)}, device_id_type=MESH
        )

    @pl.when(has_up)
    def _():
        pl.semaphore_signal(barrier, inc=1, device_id={"seq": sb + 1}, device_id_type=MESH)

    @pl.when(has_down)
    def _():
        pl.semaphore_signal(barrier, inc=1, device_id={"seq": sb - 1}, device_id_type=MESH)

    inner_block = has_up & has_down

    @pl.when(inner_block)
    def _():
        pl.semaphore_wait(barrier, n_t + 1)

    @pl.when(jnp.logical_not(inner_block))
    def _():
        pl.semaphore_wait(barrier, n_t)

    def columns(first, count):
        return pl.ds(pl.multiple_of(first * HEAD_DIM, HEAD_DIM), count * HEAD_DIM)

    def slot(owner):
        return pl.ds(pl.multiple_of(owner * rows, 16), rows)

    def sent(a, d, group, sem):
        first, count = group
        peer = lax.rem(me + d, n_t)
        return pltpu.make_async_remote_copy(
            src_ref=srcs[a].at[:, columns(peer * heads + first, count)],
            dst_ref=own.at[a, slot(me), columns(first, count)],
            send_sem=a_send.at[sem],
            recv_sem=a_recv.at[sem],
            device_id={"tensor": peer},
            device_id_type=MESH,
        )

    def sent_all(arrays, group, sem):
        first, count = group
        ref = own.at[arrays, pl.ds(0, (n_t - 1) * rows), columns(first, count)]
        return pltpu.make_async_remote_copy(
            src_ref=ref,
            dst_ref=ref,
            send_sem=a_send.at[sem],
            recv_sem=a_recv.at[sem],
            device_id={"tensor": mate},
            device_id_type=MESH,
        )

    kv_all = [sent_all(pl.ds(0, 2), g, i) for i, g in enumerate(KV_GROUPS)]
    q_all = [sent_all(pl.ds(2, 1), g, len(KV_GROUPS) + i) for i, g in enumerate(Q_GROUPS)]

    def send_kv(i):
        for a in range(2):
            for d in (3, 2, 1):
                sent(a, d, KV_GROUPS[i], i).start()

    def send_q(i):
        for d in (3, 2, 1):
            sent(2, d, Q_GROUPS[i], len(KV_GROUPS) + i).start()

    kept = [
        pltpu.make_async_copy(
            srcs[a].at[:, columns(me * heads, heads)], own.at[a, slot(me), :], a_loc.at[a]
        )
        for a in range(3)
    ]

    def edges(way, i):
        first, count = EDGE_GROUPS[i]
        by_frame = own.reshape(3, frames, 2 * span, inner_dev)
        return pltpu.make_async_remote_copy(
            src_ref=by_frame.at[
                pl.ds(0, 2), :, pl.ds(span if way == 0 else 0, span), columns(first, count)
            ],
            dst_ref=halo.at[way, :, :, :, columns(first, count)],
            send_sem=h_send.at[way, i],
            recv_sem=h_recv.at[way, i],
            device_id={"seq": sb + 1 if way == 0 else sb - 1},
            device_id_type=MESH,
        )

    def edges_start(i):
        @pl.when(has_up)
        def _():
            edges(0, i).start()

        @pl.when(has_down)
        def _():
            edges(1, i).start()

    def edges_in(i):
        @pl.when(has_down)
        def _():
            edges(0, i).wait_recv()

        @pl.when(has_up)
        def _():
            edges(1, i).wait_recv()

    def edges_out(i):
        @pl.when(has_up)
        def _():
            edges(0, i).wait_send()

        @pl.when(has_down)
        def _():
            edges(1, i).wait_send()

    def shared(kind, piece, first, count=1, part=None):
        if part is None:
            ref, at = gat.at[pl.ds(first, count), piece], first
        else:
            ref = gat.at[first, piece, pl.ds(CUTS[part], CUTS[part + 1] - CUTS[part]), :]
            at = first + part
        return pltpu.make_async_remote_copy(
            src_ref=ref,
            dst_ref=ref,
            send_sem=g_send.at[kind, at],
            recv_sem=g_recv.at[kind, at],
            device_id={"tensor": across if kind == 1 else mate},
            device_id_type=MESH,
        )

    diagonal = lax.rem(mate + n_t // 2, n_t)

    def weights_in(owner):
        return pltpu.make_async_copy(w_hbm.at[owner], wbuf.at[owner], w_sem.at[owner])

    send_kv(0)
    kept[0].start()
    kept[1].start()
    send_kv(1)
    send_kv(2)
    kept[2].start()
    consts = [
        pltpu.make_async_copy(src, dst, c_sem.at[i])
        for i, (src, dst) in enumerate(
            ((qf_hbm, qf), (kf_hbm, kf), (ext_hbm, ext_ref), (gate_hbm, gate_ref), (res_hbm, res))
        )
    ]

    @pl.when(sb == 0)
    def _():
        halo[0] = jnp.zeros(halo.shape[1:], halo.dtype)

    @pl.when(sb == n_s - 1)
    def _():
        halo[1] = jnp.zeros(halo.shape[1:], halo.dtype)

    kept[0].wait()
    kept[1].wait()
    kv_all[0].wait_recv()
    edges_start(0)
    send_q(0)
    send_kv(3)
    send_q(1)
    for copy in consts:
        copy.start()
    for owner in range(n_t):
        weights_in(owner).start()
    kv_all[1].wait_recv()
    edges_start(1)
    acc[...] = jnp.zeros_like(acc)
    kv_all[2].wait_recv()
    edges_start(2)
    edges_start(3)
    for copy in consts:
        copy.wait()
    kept[2].wait()
    for owner in range(n_t):
        weights_in(owner).wait()

    def gathered(a, h, r):
        parts = []
        for f in range(frames):
            here = own[a, f * 2 * span : (f + 1) * 2 * span, columns(h, 1)]
            there = halo[r, a, f, :, columns(h, 1)]
            parts += [there, here] if r == 0 else [here, there]
        return jnp.concatenate(parts, axis=0)

    def switches(head):
        lane = lax.broadcasted_iota(jnp.int32, (1, HEAD_DIM), 1)
        at = me * heads + head
        coef = jnp.where(lane < 8, 1.0, 0.0)
        for d, first, end in ((0, 8, 11), (2, 11, 14), (1, 14, 15)):
            stop = (1 - ext_ref[d, at]).astype(jnp.float32)
            coef = jnp.where((lane >= first) & (lane < end), stop, coef)
        coef = jnp.where(lane == 15, jnp.where(sb == 0, 1.0, 0.0), coef)
        return jnp.where(lane == 16, jnp.where(sb == n_s - 1, 1.0, 0.0), coef)

    def attend(h):
        ones = jnp.ones((frames * 3 * span, HEAD_DIM), jnp.bfloat16)
        coef = switches(h)
        for r in range(2):
            q_part = jnp.concatenate(
                [
                    own[2, (2 * f + r) * span : (2 * f + r + 1) * span, columns(h, 1)]
                    for f in range(frames)
                ],
                axis=0,
            )
            q_feat = (qf[r].astype(jnp.float32) * coef).astype(jnp.bfloat16)
            scores = lax.dot_general(
                jnp.concatenate([q_part, q_feat], axis=1),
                jnp.concatenate([gathered(0, h, r), kf[r]], axis=1),
                (((1,), (1,)), ((), ())),
                preferred_element_type=jnp.float32,
            )
            top = jnp.max(scores, axis=-1, keepdims=True)
            weights = jnp.exp2(
                (scores - top) * (math.log2(math.e) / math.sqrt(HEAD_DIM))
            ).astype(jnp.bfloat16)
            both = jnp.dot(
                weights,
                jnp.concatenate([gathered(1, h, r), ones], axis=1),
                preferred_element_type=jnp.float32,
            )
            done = (both[:, :HEAD_DIM] / both[:, HEAD_DIM:]).astype(jnp.bfloat16)
            for f in range(frames):
                gat[h, me, (2 * f + r) * span : (2 * f + r + 1) * span] = done[
                    f * span : (f + 1) * span
                ]

    def forward(first, count=1, part=None):
        if part is None:
            for h in range(first, first + count):
                shared(1, across, h).wait_recv()
        else:
            shared(1, across, first, count, part).wait_recv()
        shared(2, across, first, count, part).start()

    def product(h, base, at, cols, count=2):
        pieces = [(h + i, base + j) for i in range(count) for j in range(2)]
        lhs = jnp.concatenate([gat[i, j, at] for i, j in pieces], axis=1)
        rhs = jnp.concatenate([wbuf[j, i, :, cols] for i, j in pieces], axis=0)
        return acc[at, cols] + jnp.dot(lhs, rhs, preferred_element_type=jnp.float32)

    def accumulate(h, base):
        @pl.loop(0, acc.shape[1] // OUT_TILE)
        def _(j):
            cols = pl.ds(pl.multiple_of(j * OUT_TILE, OUT_TILE), OUT_TILE)
            acc[:, cols] = product(h, base, slice(None), cols)

    def local(h):
        shared(0, mate, h, 2).wait_recv()
        accumulate(h, near)

    def remote(h):
        shared(2, diagonal, h, 2).wait_recv()
        accumulate(h, far)

    def before(s):
        if s == 2:
            local(0)
            kv_all[3].wait_recv()
            edges_start(4)
            edges_start(5)
            edges_start(6)
            edges_start(7)
        if s == 4:
            local(2)
            for i in range(3):
                kv_all[i].wait_send()
        if s == 5:
            for i in range(3):
                edges_out(i)
            shared(0, me, 0, 2).wait_send()
            shared(0, me, 2, 2).wait_send()
        if s == 6:
            local(4)
            for i in range(2):
                q_all[i].wait_send()
            kv_all[3].wait_send()
            forward(0, 2)
        if s == 7:
            for i in range(3, 6):
                edges_out(i)
            shared(0, me, 4, 2).wait_send()
            shared(1, me, 0).wait_send()
            shared(1, me, 1).wait_send()
            remote(0)
            forward(2, 2)
            shared(2, across, 0, 2).wait_send()
        if s in (0, 2, 4):
            if s < 4:
                q_all[s // 2].wait_recv()
        for i, (first, _) in enumerate(EDGE_GROUPS):
            if first == s:
                edges_in(i)

    def after(s):
        if s < 7:
            shared(1, me, s).start()
        if s == 7:
            for part in range(PARTS):
                shared(1, me, 7, 1, part).start()
        if s % 2:
            shared(0, me, s - 1, 2).start()

    @pl.loop(0, heads)
    def _(s):
        for i in range(HEADS_DEV):
            pl.when(s == i)(functools.partial(before, i))

        attend(s)

        for i in range(HEADS_DEV):
            pl.when(s == i)(functools.partial(after, i))

    remote(2)
    forward(4, 2)
    local(6)
    shared(1, me, 2).wait_send()
    shared(1, me, 3).wait_send()
    shared(2, across, 2, 2).wait_send()
    remote(4)
    edges_out(6)
    edges_out(7)
    forward(6)
    shared(0, me, 6, 2).wait_send()
    shared(1, me, 4).wait_send()
    shared(1, me, 5).wait_send()
    shared(2, across, 4, 2).wait_send()

    def finish(part, first):
        shared(2, diagonal, 7, 1, part).wait_recv()
        at = slice(CUTS[part], CUTS[part + 1])
        for j in range(acc.shape[1] // OUT_TILE):
            cols = slice(j * OUT_TILE, (j + 1) * OUT_TILE)
            gate = gate_ref[cols].reshape(1, OUT_TILE)
            total = product(first, far, at, cols, 8 - first)
            out[at, cols] = (res[at, cols].astype(jnp.float32) + gate * total).astype(out.dtype)

    forward(7, 1, 0)
    shared(2, diagonal, 6).wait_recv()
    for part in range(1, PARTS):
        forward(7, 1, part)
        finish(part - 1, 6 if part == 1 else 7)
        if part == 1:
            at = slice(CUTS[1], CUTS[PARTS])
            for j in range(acc.shape[1] // OUT_TILE):
                cols = slice(j * OUT_TILE, (j + 1) * OUT_TILE)
                acc[at, cols] = product(6, far, at, cols, 1)
    shared(1, me, 6).wait_send()
    shared(2, across, 6).wait_send()
    for part in range(PARTS):
        shared(1, me, 7, 1, part).wait_send()
    finish(PARTS - 1, 7)
    for part in range(PARTS):
        shared(2, across, 7, 1, part).wait_send()


def put_out(src, dst, sem):
    copy = pltpu.make_async_copy(src, dst, sem)
    copy.start()
    copy.wait()


def shards(residual, queries, key_rows, value_rows, w_out, out_gate, extents):
    n_t, n_s = lax.axis_size("tensor"), lax.axis_size("seq")
    rows, inner = queries.shape
    tokens, out_cols = residual.shape
    inner_dev = inner // n_t
    heads = inner_dev // HEAD_DIM
    if n_t != 4 or n_s < 2 or rows % 16 or heads != HEADS_DEV or out_cols % OUT_TILE or rows % (4 * PARTS):
        return plain_shards(
            residual, queries, key_rows, value_rows, w_out, out_gate, extents
        )
    frames = tokens // (HT_DEV * WT * TILE)
    half = tokens // HT_DEV
    q_feat, k_feat = mask_features(frames)
    dma = pltpu.SemaphoreType.DMA
    bf16 = jnp.bfloat16
    operands = (
        queries, key_rows, value_rows, w_out.reshape(n_t, heads, HEAD_DIM, out_cols), residual,
        q_feat, k_feat, out_gate, extents.T,
    )
    result = pl.pallas_call(
        functools.partial(kernel, n_t, n_s, frames),
        out_shape=pltpu.VMEM((tokens, out_cols), bf16),
        in_specs=[pl.BlockSpec(memory_space=pl.ANY)] * len(operands),
        out_specs=pl.BlockSpec(memory_space=pltpu.VMEM),
        scratch_shapes=[
            pltpu.VMEM((3, tokens, inner_dev), bf16),
            pltpu.VMEM((2, 2, frames, half // frames, inner_dev), bf16),
            pltpu.VMEM((heads, n_t, tokens, HEAD_DIM), bf16),
            pltpu.VMEM((n_t, heads, HEAD_DIM, out_cols), bf16),
            pltpu.VMEM((tokens, out_cols), bf16),
            pltpu.VMEM((tokens, out_cols), jnp.float32),
            pltpu.VMEM(q_feat.shape, bf16),
            pltpu.VMEM(k_feat.shape, bf16),
            pltpu.VMEM(out_gate.shape, jnp.float32),
            pltpu.SMEM(extents.T.shape, jnp.int32),
            dma((len(KV_GROUPS) + len(Q_GROUPS),)),
            dma((len(KV_GROUPS) + len(Q_GROUPS),)),
            dma((3,)),
            dma((2, len(EDGE_GROUPS))),
            dma((2, len(EDGE_GROUPS))),
            dma((3, heads - 1 + PARTS)),
            dma((3, heads - 1 + PARTS)),
            dma((n_t,)),
            dma((5,)),
        ],
        compiler_params=pltpu.CompilerParams(
            collective_id=0, has_side_effects=True, vmem_limit_bytes=40 << 20
        ),
    )(*[pltpu.with_memory_space_constraint(x, pltpu.HBM) for x in operands])
    return pl.pallas_call(
        put_out,
        out_shape=jax.ShapeDtypeStruct((tokens, out_cols), bf16),
        in_specs=[pl.BlockSpec(memory_space=pl.ANY)],
        out_specs=pl.BlockSpec(memory_space=pl.ANY),
        scratch_shapes=[dma(())],
    )(pltpu.with_memory_space_constraint(result, pltpu.VMEM))


def solution(mesh):
    placed = (
        P("seq", "tensor"),
        P(("seq", "tensor"), None),
        P(("seq", "tensor"), None),
        P(("seq", "tensor"), None),
        P(None, "tensor"),
        P("tensor"),
        P(),
    )
    return jax.shard_map(
        shards, mesh=mesh, in_specs=placed, out_specs=P("seq", "tensor"), check_vma=False
    )
```
